768 devices in a mesh: dp: 64 (over y, z_hi, x), fsdp: 12 (over z_lo, core).
Axes of the slice: x: 4, y: 8, z: 12 (z_hi: 2, z_lo: 6; z = z_hi * 6 + z_lo), core: 2. Of those that a mesh axis runs over, the one named last changes fastest.
Arguments:
- z_a: bfloat16 [12288, 4224], P('dp', 'fsdp'), may hold values from -200 to 200
- z_b: bfloat16 [12288, 4224], P('dp'), may hold values from -200 to 200
Outputs:
- grad_a: bfloat16 [12288, 4224], P('dp', 'fsdp')
- grad_b: bfloat16 [12288, 4224], P('dp', 'fsdp')
The draws below stay inside these ranges and needn't reach their ends.
All inputs are finite; a program needn't handle non-finite values.
Results may differ from the reference program's by a relative error of at most 0.02.
Values may be sent and summed in bfloat16 or wider, within the bound.
A program may use at most 64 MiB of HBM per device.

```python
import math
import jax
import jax.numpy as jnp
from jax import lax

EMB = 4224
BATCH = 12288
BLOCK = 352
N_FSDP = 12


def shared_parts(key):
    base_key = jax.random.fold_in(key, 101)
    keys = jax.random.split(base_key, 5)
    classes = 32
    common = jax.random.normal(keys[0], (BATCH, EMB), jnp.float32)
    factor = jax.random.normal(keys[1], (BATCH, classes), jnp.float32)
    mixed = common + 0.8 * jnp.tile(factor, (1, EMB // classes))
    level = jax.random.uniform(keys[2], (BATCH, 1), jnp.float32)
    trend = jnp.arange(BATCH, dtype=jnp.float32)[:, None] / (BATCH - 1)
    row_scale = jnp.exp(math.log(10.0) * (level - 0.5) + math.log(3.0) * (trend - 0.5))
    col_scale = jnp.exp(jax.random.uniform(keys[3], (1, EMB), jnp.float32, minval=-1.0, maxval=1.0))
    center = 0.5 * jax.random.normal(keys[4], (1, EMB), jnp.float32)
    return (mixed, row_scale, col_scale, center)


def view_noise(key, salt):
    noise_key = jax.random.fold_in(key, salt)
    return jax.random.normal(noise_key, (BATCH, EMB), jnp.float32)


def draw_z_a(key, part):
    mixed, row_scale, col_scale, center = shared_parts(key)
    values = (mixed + 0.5 * view_noise(key, 11)) * row_scale * col_scale + center
    return values.astype(jnp.bfloat16)


def draw_z_b(key, part):
    mixed, row_scale, col_scale, center = shared_parts(key)
    values = (mixed + 0.5 * view_noise(key, 13)) * row_scale * col_scale + center
    return values.astype(jnp.bfloat16)


def setup_inputs(seed: int = 0) -> dict:
    splits = jax.random.split(jax.random.key(seed), 3)
    z_a = draw_z_a(jax.random.fold_in(splits[2], 71), 0)
    z_b = draw_z_b(jax.random.fold_in(splits[2], 71), 0)
    return dict(z_a=z_a, z_b=z_b)


eps = 1e-05
offdiag_weight = 0.0051

def normalize(values_in):
    values = values_in.astype(jnp.float32)
    center = lax.optimization_barrier(jnp.mean(values, axis=0))
    spread = lax.optimization_barrier(jnp.mean(values * values, axis=0)) - center * center
    inverse = lax.rsqrt(spread + eps)
    return ((values - center) * inverse, inverse)

def finish(back, norm, inverse):
    mean_back = lax.optimization_barrier(jnp.mean(back, axis=0))
    mean_cross = lax.optimization_barrier(jnp.mean(back * norm, axis=0))
    return (inverse * (back - mean_back - norm * mean_cross)).astype(jnp.bfloat16)

def reference(z_a, z_b):
    norm_a, inv_a = normalize(z_a)
    norm_b, inv_b = normalize(z_b)
    low_a = norm_a.astype(jnp.bfloat16)
    low_b = norm_b.astype(jnp.bfloat16)
    corr = jnp.dot(low_a.T, low_b, preferred_element_type=jnp.float32) / BATCH
    index = jnp.arange(EMB, dtype=jnp.int32)
    on_diag = index[:, None] == index[None, :]
    grad_c = jnp.where(on_diag, -2.0 * (1.0 - corr), 2.0 * offdiag_weight * corr).astype(jnp.bfloat16)
    back_a = jnp.dot(low_b, grad_c.T, preferred_element_type=jnp.float32)
    blocks_a = jnp.transpose(low_a.reshape(BATCH, N_FSDP, BLOCK), (1, 0, 2))
    blocks_g = grad_c.reshape(N_FSDP, BLOCK, EMB)

    def add_block(total, pair):
        partial_sum = jnp.dot(pair[0], pair[1], preferred_element_type=jnp.float32)
        rounded = lax.optimization_barrier(partial_sum.astype(jnp.bfloat16))
        return (total + rounded.astype(jnp.float32), None)
    back_b, _ = lax.scan(add_block, jnp.zeros((BATCH, EMB), jnp.float32), (blocks_a, blocks_g))
    return (finish(back_a, norm_a, inv_a), finish(back_b, norm_b, inv_b))
```

```python
import itertools

import jax
import jax.numpy as jnp
from jax import lax
from jax.experimental import pallas as pl
from jax.experimental.pallas import tpu as pltpu
from jax.sharding import PartitionSpec as P

EPS = 1e-05
WEIGHT = 0.0051
LANES = 128
CORES = 2
Z_HI = 2
X_CHIPS = 4
AXES = ("y", "zh", "x", "zl", "core")


def position(sizes):
    dp = lax.axis_index("dp")
    fs = lax.axis_index("fsdp")
    nx, nzh, nc = sizes["x"], sizes["zh"], sizes["core"]
    return {
        "x": dp % nx,
        "zh": (dp // nx) % nzh,
        "y": dp // (nx * nzh),
        "core": fs % nc,
        "zl": fs // nc,
    }


def device_of(place, sizes):
    dp = (place["y"] * sizes["zh"] + place["zh"]) * sizes["x"] + place["x"]
    return {"dp": dp, "fsdp": place["zl"] * sizes["core"] + place["core"]}


def exchange(src, axes, sizes, gather, collective_id):
    count = 1
    for a in axes:
        count *= sizes[a]
    piece = src.shape if gather else src.shape[1:]
    offsets = [o for o in itertools.product(*[range(sizes[a]) for a in axes]) if any(o)]

    def index(place):
        where = 0
        for a in axes:
            where = where * sizes[a] + place[a]
        return where

    def kernel(src_ref, dst_ref, send_sem, recv_sem, own_sem):
        here = position(sizes)
        me = index(here)
        peers = []
        for off in offsets:
            there = dict(here)
            for a, d in zip(axes, off):
                there[a] = (here[a] + d) % sizes[a]
            peers.append(there)
        barrier = pltpu.get_barrier_semaphore()
        for there in peers:
            pl.semaphore_signal(
                barrier,
                inc=1,
                device_id=device_of(there, sizes),
                device_id_type=pl.DeviceIdType.MESH,
            )
        own = pltpu.make_async_copy(
            src_ref if gather else src_ref.at[me], dst_ref.at[me], own_sem
        )
        own.start()
        pl.semaphore_wait(barrier, len(peers))
        copies = []
        for k, there in enumerate(peers):
            copy = pltpu.make_async_remote_copy(
                src_ref=src_ref if gather else src_ref.at[index(there)],
                dst_ref=dst_ref.at[me],
                send_sem=send_sem.at[k],
                recv_sem=recv_sem.at[k],
                device_id=device_of(there, sizes),
                device_id_type=pl.DeviceIdType.MESH,
            )
            copy.start()
            copies.append(copy)
        own.wait()
        for copy in copies:
            copy.wait()

    return pl.pallas_call(
        kernel,
        out_shape=jax.ShapeDtypeStruct((count,) + tuple(piece), src.dtype),
        in_specs=[pl.BlockSpec(memory_space=pl.ANY)],
        out_specs=pl.BlockSpec(memory_space=pl.ANY),
        scratch_shapes=[
            pltpu.SemaphoreType.DMA((len(offsets),)),
            pltpu.SemaphoreType.DMA((len(offsets),)),
            pltpu.SemaphoreType.DMA,
        ],
        compiler_params=pltpu.CompilerParams(
            collective_id=collective_id, has_side_effects=True
        ),
    )(src)


def local(z_a, z_b, sizes):
    rows, block = z_a.shape
    nx, ny, nzl, nc = sizes["x"], sizes["y"], sizes["zl"], sizes["core"]
    nf = nzl * nc
    batch = rows * nx * ny * sizes["zh"]
    lanes = -(-(block + 1) // LANES) * LANES
    per_x = nf // nx
    wide = per_x * lanes
    images = rows * nx
    slot = lanes // ny
    here = position(sizes)

    pad = ((0, 0), (0, lanes - block))
    mine = jnp.pad(z_a, pad)
    groups = []
    for x in range(nx):
        parts = [
            jnp.pad(z_b[:, f * block : (f + 1) * block], pad)
            for f in range(x * per_x, (x + 1) * per_x)
        ]
        groups.append(jnp.concatenate(parts + [mine], axis=1))
    raw = exchange(jnp.stack(groups), ("x",), sizes, False, 0).reshape(images, wide + lanes)
    raw = raw.astype(jnp.float32)

    sums = jnp.stack([jnp.sum(raw, axis=0), jnp.sum(raw * raw, axis=0)])
    every = exchange(jnp.pad(sums, ((0, 6), (0, 0))), ("y", "zh"), sizes, True, 1)
    sums = jnp.sum(every, axis=0) / batch
    center = sums[0]
    inverse = lax.rsqrt(sums[1] - center * center + EPS)
    norm = (raw - center) * inverse
    lane = jnp.arange(wide + lanes, dtype=jnp.int32) % lanes
    low = jnp.where(lane == block, 1.0, norm).astype(jnp.bfloat16)
    low_b, low_a = low[:, :wide], low[:, wide:]

    part = lax.dot_general(
        low_a, low_b, (((0,), (0,)), ((), ())), preferred_element_type=jnp.float32
    )
    got = exchange(
        part.astype(jnp.bfloat16).reshape(ny, slot, wide), ("y",), sizes, False, 2
    )
    owned = jnp.sum(got.astype(jnp.float32), axis=0)
    both = exchange(owned.astype(jnp.bfloat16), ("zh",), sizes, True, 3)
    corr = (
        owned
        + lax.dynamic_index_in_dim(both, 1 - here["zh"], 0, False).astype(jnp.float32)
    ) / batch

    row0 = (here["zl"] * nc + here["core"]) * lanes
    col0 = here["x"] * wide

    def diagonal(first_row, shape):
        row = first_row + lax.broadcasted_iota(jnp.int32, shape, 0)
        col = col0 + lax.broadcasted_iota(jnp.int32, shape, 1)
        return row == col

    grad = jnp.where(
        diagonal(row0 + here["y"] * slot, corr.shape),
        -2.0 * (1.0 - corr),
        2.0 * WEIGHT * corr,
    ).astype(jnp.bfloat16)
    grad = exchange(grad, ("y",), sizes, True, 4).reshape(lanes, wide)

    wide_g = grad.astype(jnp.float32)
    mean_b = wide_g[block, :] / (2.0 * WEIGHT)
    mean_a = wide_g[:, block] / (2.0 * WEIGHT)
    real = (lax.broadcasted_iota(jnp.int32, grad.shape, 0) < block) & (
        lax.broadcasted_iota(jnp.int32, grad.shape, 1) % lanes < block
    )
    wide_g = jnp.where(real, wide_g, 0.0)
    grad = wide_g.astype(jnp.bfloat16)
    back_corr = jnp.where(
        diagonal(row0, grad.shape), 1.0 + 0.5 * wide_g, wide_g / (2.0 * WEIGHT)
    )
    cross = wide_g * back_corr
    flat_a = jnp.sum(wide_g * mean_b[None, :], axis=1)
    flat_b = jnp.sum(wide_g * mean_a[:, None], axis=0)
    cross_a = jnp.sum(cross, axis=1)
    cross_b = jnp.sum(cross, axis=0)
    part_a = lax.dot_general(
        low_b, grad, (((1,), (1,)), ((), ())), preferred_element_type=jnp.float32
    )
    part_b = jnp.dot(low_a, grad, preferred_element_type=jnp.float32)
    part_a = part_a - flat_a - norm[:, wide:] * cross_a
    part_b = part_b - flat_b - norm[:, :wide] * cross_b
    both_parts = (jnp.concatenate([part_b, part_a], axis=1) * inverse).astype(jnp.bfloat16)
    got = exchange(
        both_parts.reshape(nx, rows, wide + lanes), ("x",), sizes, False, 5
    )
    total_a = jnp.sum(got[:, :, wide:].astype(jnp.float32), axis=0)
    grad_a = total_a[:, :block].astype(jnp.bfloat16)

    pieces = got[:, :, :wide].reshape(nx, rows, per_x, lanes)
    pieces = jnp.transpose(pieces, (0, 2, 1, 3)).reshape(nzl, nc, rows, lanes)
    pieces = jnp.transpose(pieces, (1, 0, 2, 3))
    pair = exchange(pieces, ("core",), sizes, False, 6)
    pair = jnp.sum(pair.astype(jnp.float32), axis=0).astype(jnp.bfloat16)
    line = exchange(pair, ("zl",), sizes, False, 7)
    total_b = jnp.sum(line.astype(jnp.float32), axis=0)
    grad_b = total_b[:, :block].astype(jnp.bfloat16)
    return grad_a, grad_b


def solution(mesh):
    fsdp, dp = mesh.shape["fsdp"], mesh.shape["dp"]
    sizes = {
        "core": CORES,
        "zl": fsdp // CORES,
        "x": X_CHIPS,
        "zh": Z_HI,
        "y": dp // (X_CHIPS * Z_HI),
    }
    return jax.shard_map(
        lambda z_a, z_b: local(z_a, z_b, sizes),
        mesh=mesh,
        in_specs=(P("dp", "fsdp"), P("dp", None)),
        out_specs=(P("dp", "fsdp"), P("dp", "fsdp")),
        check_vma=False,
    )
```

```python
import jax
import jax.numpy as jnp
from jax import lax
from jax.experimental import pallas as pl
from jax.experimental.pallas import tpu as pltpu
from jax.sharding import PartitionSpec as P

EPS = 1e-05
WEIGHT = 0.0051
LANES = 128
CORES = 2
Z_HI = 2
X_CHIPS = 4
SUB = 4
MESH = pl.DeviceIdType.MESH
F32 = jnp.float32
BF16 = jnp.bfloat16


class Plan:
    def __init__(self, mesh, rows, block):
        fsdp, dp = mesh.shape["fsdp"], mesh.shape["dp"]
        self.nx, self.nh, self.nc = X_CHIPS, Z_HI, CORES
        self.ny = dp // (self.nx * self.nh)
        self.nz = fsdp // self.nc
        self.nf = fsdp
        self.nq = self.nf // self.nx
        self.rows, self.block = rows, block
        self.lanes = -(-(block + 1) // LANES) * LANES
        self.slot = self.lanes // self.ny
        self.batch = rows * dp
        self.right = self.ny // 2
        self.left = self.ny - 1 - self.right


class Copies:
    def __init__(self):
        self.count = 0

    def take(self, n=1):
        first = self.count
        self.count += n
        return first


def build(p):
    copies = Copies()
    nx, ny, nh, nz, nc, nq = p.nx, p.ny, p.nh, p.nz, p.nc, p.nq
    rows, lanes, slot, block = p.rows, p.lanes, p.slot, p.block
    half = rows // nc
    part = rows // SUB
    marks = dict(
        a=copies.take(nx),
        b=copies.take(nx * nq),
        pass_b=copies.take(nx * nq),
        stat_x=copies.take(nx),
        stat_y=copies.take(ny),
        stat_h=copies.take(nh),
        rs_r=copies.take(p.right * nq),
        rs_l=copies.take(p.left * nq),
        swap=copies.take(nq),
        ag_r=copies.take(p.right * nq),
        ag_l=copies.take(p.left * nq),
        pair=copies.take((nx // nc) * nq),
        back_a=copies.take(nx),
        chain_r=copies.take(nz * SUB),
        chain_l=copies.take(nz * SUB),
        final=copies.take(1),
    )

    def kernel(
        za,
        zb,
        out_a,
        out_b,
        raw_a,
        raw_b,
        pack,
        low_a,
        low_b,
        low_t,
        stat_x,
        stat_y,
        stat_h,
        mean,
        tile,
        rs_rin,
        rs_rout,
        rs_lin,
        rs_lout,
        owned,
        swap_out,
        swap_in,
        grad,
        acc_a,
        send_a,
        recv_a,
        blocks,
        pair,
        chain_rin,
        chain_rout,
        chain_lin,
        chain_lout,
        done_out,
        done_in,
        send_sem,
        recv_sem,
        own_sem,
    ):
        dp = lax.axis_index("dp")
        fs = lax.axis_index("fsdp")
        x = dp % nx
        h = (dp // nx) % nh
        y = dp // (nx * nh)
        core = fs % nc
        zl = fs // nc

        def device(x=x, y=y, h=h, zl=zl, core=core):
            return {"dp": (y * nh + h) * nx + x, "fsdp": zl * nc + core}

        def remote(src, dst, mark, there):
            return pltpu.make_async_remote_copy(
                src_ref=src,
                dst_ref=dst,
                send_sem=send_sem.at[mark],
                recv_sem=recv_sem.at[mark],
                device_id=there,
                device_id_type=MESH,
            )

        q_own = zl % nq
        to_x = (zl // nq) * nc + core
        to_f = nq * x + q_own
        from_x = fs // nq
        from_q = fs % nq
        from_z = (x // nc) * nq + from_q
        stays = (to_x == x) & (to_f == fs)

        barrier = pltpu.get_barrier_semaphore()

        def greet(there):
            pl.semaphore_signal(barrier, inc=1, device_id=there, device_id_type=MESH)

        for k in range(1, nx):
            greet(device(x=(x + k) % nx))
        for k in range(1, ny):
            greet(device(y=(y + k) % ny))
        greet(device(h=1 - h))
        greet(device(core=1 - core))
        greet(device(zl=(zl + 1) % nz))
        greet(device(zl=(zl + nz - 1) % nz))

        @pl.when(jnp.logical_not(stays))
        def _():
            greet(device(x=from_x, zl=from_z, core=x % nc))

        waiting = []

        zero = jnp.zeros((rows, lanes - block), BF16)
        raw_a[x] = jnp.concatenate([za[...], zero], axis=1)
        for f in range(p.nf):
            piece = zb[:, f * block : (f + 1) * block]
            pack[f // nq, f % nq] = jnp.concatenate([piece, zero], axis=1)

        pl.semaphore_wait(barrier, nx - 1 + ny - 1 + 4 + jnp.where(stays, 0, 1))

        def start(copy):
            copy.start()
            waiting.append(copy)
            return copy

        into_a = {}
        for k in range(1, nx):
            into_a[k] = start(
                remote(
                    raw_a.at[x], raw_a.at[x], marks["a"] + k, device(x=(x + k) % nx)
                )
            )
        own_rows = pl.ds(core * half, half)
        into_b = {}
        for q in range(nq):
            for k in range(1, nx):
                t = (x + k) % nx
                into_b[q, k] = start(
                    remote(
                        pack.at[t, q, own_rows],
                        raw_b.at[q, x, own_rows],
                        marks["b"] + q * nx + k,
                        device(x=t),
                    )
                )
        mine = []
        for q in range(nq):
            copy = pltpu.make_async_copy(pack.at[x, q], raw_b.at[q, x], own_sem.at[q])
            copy.start()
            mine.append(copy)

        def sums(value):
            v = value.astype(F32)
            return (
                jnp.sum(v, axis=0, keepdims=True),
                jnp.sum(v * v, axis=0, keepdims=True),
            )

        first = [sums(pack[f // nq, f % nq]) for f in range(p.nf)]
        first_a = sums(raw_a[x])
        for t in range(nx):
            both = first[t * nq : (t + 1) * nq] + [first_a]
            stat_x[0, t] = jnp.concatenate(
                [s for s, _ in both] + [s for _, s in both], axis=0
            )
        got = []
        for k in range(1, nx):
            t = (x + k) % nx
            got.append(
                start(
                    remote(
                        stat_x.at[0, t],
                        stat_x.at[1, k],
                        marks["stat_x"] + k,
                        device(x=t),
                    )
                )
            )
        total = stat_x[0, x]
        for k in range(1, nx):
            got[k - 1].wait_recv()
            total = total + stat_x[1, k]
        stat_y[0] = total
        got = []
        for k in range(1, ny):
            got.append(
                start(
                    remote(
                        stat_y.at[0],
                        stat_y.at[k],
                        marks["stat_y"] + k,
                        device(y=(y + k) % ny),
                    )
                )
            )
        for k in range(1, ny):
            got[k - 1].wait_recv()
            total = total + stat_y[k]
        stat_h[0] = total
        swap = start(
            remote(stat_h.at[0], stat_h.at[1], marks["stat_h"], device(h=1 - h))
        )
        swap.wait_recv()
        total = (total + stat_h[1]) / p.batch
        count = nq + 1
        center = total[:count]
        inverse = lax.rsqrt(total[count:] - center * center + EPS)
        mean[:count] = center
        mean[count:] = inverse

        lane = lax.broadcasted_iota(jnp.int32, (rows, lanes), 1)

        def normal(raw, which):
            v = raw.astype(F32)
            return (v - mean[which : which + 1, :]) * mean[
                count + which : count + which + 1, :
            ]

        def low(raw, which):
            return jnp.where(lane == block, 1.0, normal(raw, which)).astype(BF16)

        for k in range(1, nx):
            into_a[k].wait_recv()

        def low_a_step(i, _):
            low_a[i] = low(raw_a[i], nq)
            return 0

        lax.fori_loop(0, nx, low_a_step, 0)
        for i in range(nx):
            low_t[:, i * rows : (i + 1) * rows] = jnp.transpose(
                low_a[i].astype(F32)
            ).astype(BF16)

        passed = {}
        for q in range(nq):
            for k in range(1, nx):
                into_b[q, k].wait_recv()
                s = (x + nx - k) % nx
                passed[q, k] = start(
                    remote(
                        raw_b.at[q, s, own_rows],
                        raw_b.at[q, s, own_rows],
                        marks["pass_b"] + q * nx + k,
                        device(core=1 - core),
                    )
                )

        right, left = device(y=(y + 1) % ny), device(y=(y + ny - 1) % ny)

        def ring(src, dst, name, step, q, there):
            return start(remote(src, dst, marks[name] + step * nq + q, there))

        rs_r, rs_l = {}, {}
        for q in range(nq):
            mine[q].wait()
            for k in range(1, nx):
                passed[q, k].wait_recv()

            def low_b_step(i, _):
                low_b[q, i] = low(raw_b[q, i], q)
                return 0

            lax.fori_loop(0, nx, low_b_step, 0)
            product = jnp.dot(
                low_t[...],
                low_b[q].reshape(nx * rows, lanes),
                preferred_element_type=F32,
            )
            tile[q] = product.astype(BF16).reshape(ny, slot, lanes)
            rs_r[0, q] = ring(
                tile.at[q, (y + p.right) % ny], rs_rin.at[0, q], "rs_r", 0, q, right
            )
            rs_l[0, q] = ring(
                tile.at[q, (y + ny - p.left) % ny], rs_lin.at[0, q], "rs_l", 0, q, left
            )

        for s in range(1, p.right):
            for q in range(nq):
                t = (y + p.right - s) % ny
                rs_r[s - 1, q].wait_recv()
                rs_rout[s, q] = (
                    rs_rin[s - 1, q].astype(F32) + tile[q, t].astype(F32)
                ).astype(BF16)
                rs_r[s, q] = ring(
                    rs_rout.at[s, q], rs_rin.at[s, q], "rs_r", s, q, right
                )
                if s < p.left:
                    t = (y + ny - p.left + s) % ny
                    rs_l[s - 1, q].wait_recv()
                    rs_lout[s, q] = (
                        rs_lin[s - 1, q].astype(F32) + tile[q, t].astype(F32)
                    ).astype(BF16)
                    rs_l[s, q] = ring(
                        rs_lout.at[s, q], rs_lin.at[s, q], "rs_l", s, q, left
                    )
        swaps = {}
        for q in range(nq):
            rs_l[p.left - 1, q].wait_recv()
            rs_r[p.right - 1, q].wait_recv()
            value = (
                tile[q, y].astype(F32)
                + rs_rin[p.right - 1, q].astype(F32)
                + rs_lin[p.left - 1, q].astype(F32)
            )
            owned[q] = value
            swap_out[q] = value.astype(BF16)
            swaps[q] = start(
                remote(
                    swap_out.at[q], swap_in.at[q], marks["swap"] + q, device(h=1 - h)
                )
            )

        ag_r, ag_l = {}, {}
        for q in range(nq):
            swaps[q].wait_recv()
            corr = (owned[q] + swap_in[q].astype(F32)) / p.batch
            row = y * slot + lax.broadcasted_iota(jnp.int32, (slot, lanes), 0)
            col = lax.broadcasted_iota(jnp.int32, (slot, lanes), 1)
            on = (row == col) & (fs == nq * x + q)
            grad[q, y] = jnp.where(
                on, -2.0 * (1.0 - corr), 2.0 * WEIGHT * corr
            ).astype(BF16)
            ag_r[0, q] = ring(grad.at[q, y], grad.at[q, y], "ag_r", 0, q, right)
            ag_l[0, q] = ring(grad.at[q, y], grad.at[q, y], "ag_l", 0, q, left)
        for s in range(1, p.right):
            for q in range(nq):
                ag_r[s - 1, q].wait_recv()
                t = (y + ny - s) % ny
                ag_r[s, q] = ring(grad.at[q, t], grad.at[q, t], "ag_r", s, q, right)
                if s < p.left:
                    ag_l[s - 1, q].wait_recv()
                    t = (y + s) % ny
                    ag_l[s, q] = ring(grad.at[q, t], grad.at[q, t], "ag_l", s, q, left)
        for q in range(nq):
            ag_r[p.right - 1, q].wait_recv()
            ag_l[p.left - 1, q].wait_recv()

        row = lax.broadcasted_iota(jnp.int32, (lanes, lanes), 0)
        col = lax.broadcasted_iota(jnp.int32, (lanes, lanes), 1)
        real = (row < block) & (col < block)
        flat_a = jnp.zeros((1, lanes), F32)
        cross_a = jnp.zeros((1, lanes), F32)
        pairs = {}
        for q in range(nq):
            g = grad[q].reshape(lanes, lanes).astype(F32)
            mean_b = g[block : block + 1, :] / (2.0 * WEIGHT)
            mean_a = g[:, block : block + 1] / (2.0 * WEIGHT)
            g = jnp.where(real, g, 0.0)
            on = (row == col) & (fs == nq * x + q)
            cross = g * jnp.where(on, 1.0 + 0.5 * g, g / (2.0 * WEIGHT))
            flat_b = jnp.sum(g * mean_a, axis=0, keepdims=True)
            cross_b = jnp.sum(cross, axis=0, keepdims=True)
            flat_a += jnp.sum(jnp.transpose(g * mean_b), axis=0, keepdims=True)
            cross_a += jnp.sum(jnp.transpose(cross), axis=0, keepdims=True)
            g = g.astype(BF16)

            def back_b_step(i, _):
                value = jnp.dot(low_a[i], g, preferred_element_type=F32)
                value = value - flat_b - normal(raw_b[q, i], q) * cross_b
                blocks[i, q] = (value * mean[count + q : count + q + 1, :]).astype(BF16)
                return 0

            lax.fori_loop(0, nx, back_b_step, 0)
            for m in range(nx // nc):
                pairs[m, q] = start(
                    remote(
                        blocks.at[m * nc + 1 - core, q],
                        pair.at[m, q],
                        marks["pair"] + m * nq + q,
                        device(core=1 - core),
                    )
                )

            def back_a_step(i, _):
                value = lax.dot_general(
                    low_b[q, i], g, (((1,), (1,)), ((), ())), preferred_element_type=F32
                )
                acc_a[i] = value if q == 0 else acc_a[i] + value
                return 0

            lax.fori_loop(0, nx, back_a_step, 0)

        inv_a = mean[count + nq : count + nq + 1, :]

        def close_a_step(i, _):
            value = acc_a[i] - flat_a - normal(raw_a[i], nq) * cross_a
            value = value * inv_a
            acc_a[i] = value
            send_a[i] = value.astype(BF16)
            return 0

        lax.fori_loop(0, nx, close_a_step, 0)
        backs = []
        for k in range(1, nx):
            t = (x + k) % nx
            backs.append(
                start(
                    remote(
                        send_a.at[t], recv_a.at[k], marks["back_a"] + k, device(x=t)
                    )
                )
            )
        for m in range(nx // nc):
            for q in range(nq):
                pairs[m, q].wait_recv()

        def own(d, s):
            m, q = d // nq, d % nq
            at = pl.ds(s * part, part)
            return blocks[m * nc + core, q, at].astype(F32) + pair[m, q, at].astype(F32)

        def hop(src, dst, name, d, s, step):
            return remote(
                src.at[d, s],
                dst.at[d, s],
                marks[name] + d * SUB + s,
                device(zl=(zl + step + nz) % nz),
            )

        def hop_r(d, s):
            return hop(chain_rout, chain_rin, "chain_r", d, s, 1)

        def hop_l(d, s):
            return hop(chain_lout, chain_lin, "chain_l", d, s, -1)

        def chain(make, inbox, outbox, target, steps, starts):
            def step(i, _):
                d = target(i)
                for s in range(SUB):

                    @pl.when(starts)
                    def _():
                        outbox[d, s] = own(d, s).astype(BF16)

                    @pl.when(jnp.logical_not(starts))
                    def _():
                        make(d, s).wait_recv()
                        outbox[d, s] = (own(d, s) + inbox[d, s].astype(F32)).astype(
                            BF16
                        )

                    make(d, s).start()
                return 0

            lax.fori_loop(0, steps, step, 0)

        def chain_end(make, target, steps):
            def step(i, _):
                for s in range(SUB):
                    make(target(i), s).wait_send()
                return 0

            lax.fori_loop(0, steps, step, 0)

        def chain_right():
            chain(
                hop_r,
                chain_rin,
                chain_rout,
                lambda i: nz - 1 - i,
                nz - 1 - zl,
                zl == 0,
            )

        def chain_left():
            chain(hop_l, chain_lin, chain_lout, lambda i: i, zl, zl == nz - 1)

        low_half = zl < nz // 2

        @pl.when(low_half)
        def _():
            chain_right()
            chain_left()

        @pl.when(jnp.logical_not(low_half))
        def _():
            chain_left()
            chain_right()

        total_a = acc_a[x]
        for k in range(1, nx):
            backs[k - 1].wait_recv()
            total_a = total_a + recv_a[k].astype(F32)
        out_a[...] = total_a[:, :block].astype(BF16)

        for s in range(SUB):
            at = pl.ds(s * part, part)
            acc_a[0, at] = own(zl, s)

            @pl.when(zl > 0)
            def _():
                hop_r(zl, s).wait_recv()
                acc_a[0, at] += chain_rin[zl, s].astype(F32)

            @pl.when(zl < nz - 1)
            def _():
                hop_l(zl, s).wait_recv()
                acc_a[0, at] += chain_lin[zl, s].astype(F32)

        done_out[...] = acc_a[0].astype(BF16)
        last = remote(
            done_out,
            done_in,
            marks["final"],
            device(x=to_x, zl=to_f // nc, core=to_f % nc),
        )

        @pl.when(stays)
        def _():
            out_b[...] = done_out[:, :block]

        @pl.when(jnp.logical_not(stays))
        def _():
            last.start()
            last.wait()
            out_b[...] = done_in[:, :block]

        chain_end(hop_r, lambda i: nz - 1 - i, nz - 1 - zl)
        chain_end(hop_l, lambda i: i, zl)
        for copy in waiting:
            copy.wait_send()

    vmem = pltpu.VMEM
    count = nq + 1
    shapes = [
        vmem((nx, rows, lanes), BF16),
        vmem((nq, nx, rows, lanes), BF16),
        vmem((nx, nq, rows, lanes), BF16),
        vmem((nx, rows, lanes), BF16),
        vmem((nq, nx, rows, lanes), BF16),
        vmem((lanes, nx * rows), BF16),
        vmem((2, nx, 2 * count, lanes), F32),
        vmem((ny, 2 * count, lanes), F32),
        vmem((2, 2 * count, lanes), F32),
        vmem((2 * count, lanes), F32),
        vmem((nq, ny, slot, lanes), BF16),
        vmem((p.right, nq, slot, lanes), BF16),
        vmem((p.right, nq, slot, lanes), BF16),
        vmem((max(p.left, 1), nq, slot, lanes), BF16),
        vmem((max(p.left, 1), nq, slot, lanes), BF16),
        vmem((nq, slot, lanes), F32),
        vmem((nq, slot, lanes), BF16),
        vmem((nq, slot, lanes), BF16),
        vmem((nq, ny, slot, lanes), BF16),
        vmem((nx, rows, lanes), F32),
        vmem((nx, rows, lanes), BF16),
        vmem((nx, rows, lanes), BF16),
        vmem((nx, nq, rows, lanes), BF16),
        vmem((nx // nc, nq, rows, lanes), BF16),
        vmem((nz, SUB, part, lanes), BF16),
        vmem((nz, SUB, part, lanes), BF16),
        vmem((nz, SUB, part, lanes), BF16),
        vmem((nz, SUB, part, lanes), BF16),
        vmem((rows, lanes), BF16),
        vmem((rows, lanes), BF16),
        pltpu.SemaphoreType.DMA((copies.count,)),
        pltpu.SemaphoreType.DMA((copies.count,)),
        pltpu.SemaphoreType.DMA((nq,)),
    ]
    result = jax.ShapeDtypeStruct((rows, block), BF16)
    return pl.pallas_call(
        kernel,
        out_shape=(result, result),
        in_specs=[pl.BlockSpec(memory_space=vmem)] * 2,
        out_specs=(pl.BlockSpec(memory_space=vmem),) * 2,
        scratch_shapes=shapes,
        compiler_params=pltpu.CompilerParams(
            collective_id=0, has_side_effects=True, vmem_limit_bytes=56 << 20
        ),
    )


def solution(mesh):
    def local(z_a, z_b):
        return build(Plan(mesh, *z_a.shape))(z_a, z_b)

    return jax.shard_map(
        local,
        mesh=mesh,
        in_specs=(P("dp", "fsdp"), P("dp", None)),
        out_specs=(P("dp", "fsdp"), P("dp", "fsdp")),
        check_vma=False,
    )
```

```python
import jax
import jax.numpy as jnp
from jax import lax
from jax.experimental import pallas as pl
from jax.experimental.pallas import tpu as pltpu
from jax.sharding import PartitionSpec as P

EPS = 1e-05
WEIGHT = 0.0051
LANES = 128
CORES = 2
Z_HI = 2
X_CHIPS = 4
SUB = 4
MESH = pl.DeviceIdType.MESH
F32 = jnp.float32
BF16 = jnp.bfloat16


class Plan:
    def __init__(self, mesh, rows, block):
        fsdp, dp = mesh.shape["fsdp"], mesh.shape["dp"]
        self.nx, self.nh, self.nc = X_CHIPS, Z_HI, CORES
        self.ny = dp // (self.nx * self.nh)
        self.nz = fsdp // self.nc
        self.nf = fsdp
        self.nq = self.nf // self.nx
        self.rows, self.block = rows, block
        self.lanes = -(-(block + 1) // LANES) * LANES
        self.slot = self.lanes // self.ny
        self.batch = rows * dp
        right = self.ny // 2
        self.routes = []
        for step, reach in ((1, right), (-1, self.ny - 1 - right)):
            for near in range(1, reach + 1, 2):
                self.routes.append((step, near, near < reach))


class Copies:
    def __init__(self):
        self.count = 0

    def take(self, n=1):
        first = self.count
        self.count += n
        return first


def build(p):
    copies = Copies()
    nx, ny, nh, nz, nc, nq = p.nx, p.ny, p.nh, p.nz, p.nc, p.nq
    rows, lanes, slot, block = p.rows, p.lanes, p.slot, p.block
    half = rows // nc
    quarter = half // 2
    part = rows // SUB
    routes = p.routes
    pairs_x = nx // nc
    marks = dict(
        a=copies.take(nx),
        b=copies.take(nx * nq),
        pass_z=copies.take(nx * nq),
        pass_c=copies.take(nx * nq),
        stat_x=copies.take(nx),
        stat_y=copies.take(ny),
        stat_h=copies.take(nh),
        mid=copies.take(len(routes) * nq),
        fin=copies.take(len(routes) * nq),
        swap=copies.take(nq),
        near=copies.take(len(routes) * nq),
        far=copies.take(len(routes) * nq),
        pair=copies.take(pairs_x * nq),
        back_a=copies.take(nx),
        scatter=copies.take(max(pairs_x, nx) * nq),
        chain=copies.take(3 * nz * SUB),
    )

    def kernel(
        za,
        zb,
        out_a,
        out_b,
        raw_a,
        raw_b,
        pack,
        low_a,
        low_b,
        low_t,
        stat_x,
        stat_y,
        stat_h,
        mean,
        tile,
        mid_in,
        mid_out,
        fin_in,
        owned,
        swap_out,
        swap_in,
        grad,
        acc_a,
        send_a,
        recv_a,
        blocks,
        pair,
        scatter_out,
        line,
        chain_in,
        chain_out,
        owned_b,
        send_sem,
        recv_sem,
        own_sem,
    ):
        dp = lax.axis_index("dp")
        fs = lax.axis_index("fsdp")
        x = dp % nx
        h = (dp // nx) % nh
        y = dp // (nx * nh)
        core = fs % nc
        zl = fs // nc

        def device(x=x, y=y, h=h, zl=zl, core=core):
            return {"dp": (y * nh + h) * nx + x, "fsdp": zl * nc + core}

        def remote(src, dst, mark, there, recv_mark=None):
            arrived = mark if recv_mark is None else recv_mark
            return pltpu.make_async_remote_copy(
                src_ref=src,
                dst_ref=dst,
                send_sem=send_sem.at[mark],
                recv_sem=recv_sem.at[arrived],
                device_id=there,
                device_id_type=MESH,
            )

        barrier = pltpu.get_barrier_semaphore()

        def greet(there):
            pl.semaphore_signal(barrier, inc=1, device_id=there, device_id_type=MESH)

        greet(device(core=1 - core))
        for k in range(1, nx):
            greet(device(x=(x + k) % nx))
            greet(device(x=(x + k) % nx, core=1 - core))
        for k in range(1, ny):
            greet(device(y=(y + k) % ny))
        greet(device(h=1 - h))
        for k in range(1, nz):
            greet(device(zl=(zl + k) % nz))

        waiting = []

        zero = jnp.zeros((rows, lanes - block), BF16)
        raw_a[x] = jnp.concatenate([za[...], zero], axis=1)
        for f in range(p.nf):
            piece = zb[:, f * block : (f + 1) * block]
            pack[f // nq, f % nq] = jnp.concatenate([piece, zero], axis=1)

        def sums(value):
            v = value.astype(F32)
            return (
                jnp.sum(v, axis=0, keepdims=True),
                jnp.sum(v * v, axis=0, keepdims=True),
            )

        first = [sums(pack[f // nq, f % nq]) for f in range(p.nf)]
        first_a = sums(raw_a[x])
        for t in range(nx):
            both = first[t * nq : (t + 1) * nq] + [first_a]
            stat_x[0, t] = jnp.concatenate(
                [s for s, _ in both] + [s for _, s in both], axis=0
            )

        pl.semaphore_wait(barrier, 2 * (nx - 1) + ny - 1 + nz - 1 + 2)

        def start(copy):
            copy.start()
            waiting.append(copy)
            return copy

        got_x, got_y = {}, {}
        for k in range(1, nx):
            t = (x + k) % nx
            got_x[k] = start(
                remote(
                    stat_x.at[0, t],
                    stat_x.at[1, k],
                    marks["stat_x"] + k,
                    device(x=t),
                )
            )
        into_a = {}
        for k in range(1, nx):
            into_a[k] = start(
                remote(
                    raw_a.at[x], raw_a.at[x], marks["a"] + k, device(x=(x + k) % nx)
                )
            )
        own_rows = pl.ds(core * half + (zl % 2) * quarter, quarter)
        core_rows = pl.ds(core * half, half)
        z_pair = device(zl=zl + 1 - 2 * (zl % 2))
        into_b = {}
        for q in range(nq):
            for k in range(1, nx):
                t = (x + k) % nx
                into_b[q, k] = start(
                    remote(
                        pack.at[t, q, own_rows],
                        raw_b.at[q, x, own_rows],
                        marks["b"] + q * nx + k,
                        device(x=t),
                    )
                )
        mine = []
        for q in range(nq):
            copy = pltpu.make_async_copy(pack.at[x, q], raw_b.at[q, x], own_sem.at[q])
            copy.start()
            mine.append(copy)

        total = stat_x[0, x]
        for k in range(1, nx):
            got_x[k].wait_recv()
            total = total + stat_x[1, k]
        stat_y[0] = total
        for k in range(1, ny):
            got_y[k] = start(
                remote(
                    stat_y.at[0],
                    stat_y.at[k],
                    marks["stat_y"] + k,
                    device(y=(y + k) % ny),
                )
            )
        for k in range(1, ny):
            got_y[k].wait_recv()
            total = total + stat_y[k]
        stat_h[0] = total
        other = start(
            remote(stat_h.at[0], stat_h.at[1], marks["stat_h"], device(h=1 - h))
        )
        other.wait_recv()
        total = (total + stat_h[1]) / p.batch
        count = nq + 1
        center = total[:count]
        inverse = lax.rsqrt(total[count:] - center * center + EPS)
        mean[:count] = center
        mean[count:] = inverse

        lane = lax.broadcasted_iota(jnp.int32, (rows, lanes), 1)

        def normal(raw, which):
            v = raw.astype(F32)
            return (v - mean[which : which + 1, :]) * mean[
                count + which : count + which + 1, :
            ]

        def low(raw, which):
            return jnp.where(lane == block, 1.0, normal(raw, which)).astype(BF16)

        for k in range(1, nx):
            into_a[k].wait_recv()

        def low_a_step(i, _):
            low_a[i] = low(raw_a[i], nq)
            return 0

        lax.fori_loop(0, nx, low_a_step, 0)
        for i in range(nx):
            low_t[:, i * rows : (i + 1) * rows] = jnp.transpose(
                low_a[i].astype(F32)
            ).astype(BF16)

        passed_z, passed, swaps, pairs = {}, {}, {}, {}
        mid, fin, near_ag, far_ag = {}, {}, {}, {}

        def pass_z(q):
            for k in range(1, nx):
                into_b[q, k].wait_recv()
                s = (x + nx - k) % nx
                passed_z[q, k] = start(
                    remote(
                        raw_b.at[q, s, own_rows],
                        raw_b.at[q, s, own_rows],
                        marks["pass_z"] + q * nx + k,
                        z_pair,
                    )
                )

        def pass_core(q):
            for k in range(1, nx):
                passed_z[q, k].wait_recv()
                s = (x + nx - k) % nx
                passed[q, k] = start(
                    remote(
                        raw_b.at[q, s, core_rows],
                        raw_b.at[q, s, core_rows],
                        marks["pass_c"] + q * nx + k,
                        device(core=1 - core),
                    )
                )

        def along(distance):
            return (y + distance + ny) % ny

        def make_tile(q):
            mine[q].wait()
            for k in range(1, nx):
                passed[q, k].wait_recv()

            def low_b_step(i, _):
                low_b[q, i] = low(raw_b[q, i], q)
                return 0

            lax.fori_loop(0, nx, low_b_step, 0)
            product = jnp.dot(
                low_t[...],
                low_b[q].reshape(nx * rows, lanes),
                preferred_element_type=F32,
            )
            tile[q] = product.astype(BF16).reshape(ny, slot, lanes)
            for r, (step, near, goes_on) in enumerate(routes):
                mark = r * nq + q
                if goes_on:
                    t = along(step * (near + 1))
                    mid[r, q] = start(
                        remote(
                            tile.at[q, t],
                            mid_in.at[r, q],
                            marks["mid"] + mark,
                            device(y=along(step)),
                        )
                    )
                else:
                    t = along(step * near)
                    fin[r, q] = start(
                        remote(
                            tile.at[q, t],
                            fin_in.at[r, q],
                            marks["fin"] + mark,
                            device(y=t),
                        )
                    )

        def sum_step(q):
            for r, (step, near, goes_on) in enumerate(routes):
                if goes_on:
                    t = along(step * near)
                    mid[r, q].wait_recv()
                    mid_out[r, q] = (
                        mid_in[r, q].astype(F32) + tile[q, t].astype(F32)
                    ).astype(BF16)
                    fin[r, q] = start(
                        remote(
                            mid_out.at[r, q],
                            fin_in.at[r, q],
                            marks["fin"] + r * nq + q,
                            device(y=t),
                        )
                    )

        def swap_step(q):
            value = tile[q, y].astype(F32)
            for r in range(len(routes)):
                fin[r, q].wait_recv()
                value = value + fin_in[r, q].astype(F32)
            owned[q] = value
            swap_out[q] = value.astype(BF16)
            swaps[q] = start(
                remote(
                    swap_out.at[q], swap_in.at[q], marks["swap"] + q, device(h=1 - h)
                )
            )

        def grad_step(q):
            swaps[q].wait_recv()
            corr = (owned[q] + swap_in[q].astype(F32)) / p.batch
            row = y * slot + lax.broadcasted_iota(jnp.int32, (slot, lanes), 0)
            col = lax.broadcasted_iota(jnp.int32, (slot, lanes), 1)
            on = (row == col) & (fs == nq * x + q)
            grad[q, y] = jnp.where(
                on, -2.0 * (1.0 - corr), 2.0 * WEIGHT * corr
            ).astype(BF16)
            for r, (step, near, goes_on) in enumerate(routes):
                near_ag[r, q] = start(
                    remote(
                        grad.at[q, y],
                        grad.at[q, y],
                        marks["near"] + r * nq + q,
                        device(y=along(step * near)),
                    )
                )

        def gather_step(q):
            for r, (step, near, goes_on) in enumerate(routes):
                near_ag[r, q].wait_recv()
                if goes_on:
                    t = along(-step * near)
                    far_ag[r, q] = start(
                        remote(
                            grad.at[q, t],
                            grad.at[q, t],
                            marks["far"] + r * nq + q,
                            device(y=along(step)),
                        )
                    )

        means_a = [jnp.zeros((1, lanes), F32), jnp.zeros((1, lanes), F32)]

        def back_step(q):
            for r, (step, near, goes_on) in enumerate(routes):
                if goes_on:
                    far_ag[r, q].wait_recv()
            row = lax.broadcasted_iota(jnp.int32, (lanes, lanes), 0)
            col = lax.broadcasted_iota(jnp.int32, (lanes, lanes), 1)
            g = grad[q].reshape(lanes, lanes).astype(F32)
            mean_b = g[block : block + 1, :] / (2.0 * WEIGHT)
            mean_a = g[:, block : block + 1] / (2.0 * WEIGHT)
            g = jnp.where((row < block) & (col < block), g, 0.0)
            on = (row == col) & (fs == nq * x + q)
            cross = g * jnp.where(on, 1.0 + 0.5 * g, g / (2.0 * WEIGHT))
            flat_b = jnp.sum(g * mean_a, axis=0, keepdims=True)
            cross_b = jnp.sum(cross, axis=0, keepdims=True)
            low_g = g.astype(BF16)

            def back_b_step(i, _):
                value = jnp.dot(low_a[i], low_g, preferred_element_type=F32)
                value = value - flat_b - normal(raw_b[q, i], q) * cross_b
                blocks[i, q] = (value * mean[count + q : count + q + 1, :]).astype(BF16)
                return 0

            lax.fori_loop(0, nx, back_b_step, 0)
            for m in range(nx // nc):
                pairs[m, q] = start(
                    remote(
                        blocks.at[m * nc + 1 - core, q],
                        pair.at[m, q],
                        marks["pair"] + m * nq + q,
                        device(core=1 - core),
                    )
                )

            means_a[0] += jnp.sum(jnp.transpose(g * mean_b), axis=0, keepdims=True)
            means_a[1] += jnp.sum(jnp.transpose(cross), axis=0, keepdims=True)

            def back_a_step(i, _):
                value = lax.dot_general(
                    low_b[q, i],
                    low_g,
                    (((1,), (1,)), ((), ())),
                    preferred_element_type=F32,
                )
                acc_a[i] = value if q == 0 else acc_a[i] + value
                return 0

            lax.fori_loop(0, nx, back_a_step, 0)

        backs = {}

        def close_a():
            inv_a = mean[count + nq : count + nq + 1, :]

            def close_a_step(i, _):
                value = acc_a[i] - means_a[0] - normal(raw_a[i], nq) * means_a[1]
                value = value * inv_a
                acc_a[i] = value
                send_a[i] = value.astype(BF16)
                return 0

            lax.fori_loop(0, nx, close_a_step, 0)
            for k in range(1, nx):
                t = (x + k) % nx
                backs[k] = start(
                    remote(
                        send_a.at[t], recv_a.at[k], marks["back_a"] + k, device(x=t)
                    )
                )

        mine_f = [nq * x + q for q in range(nq)]

        def scatter_copy(m, q):
            return remote(
                scatter_out.at[m, q],
                line.at[mine_f[q] // nc],
                marks["scatter"] + q * pairs_x + m,
                device(x=m * nc + core, core=mine_f[q] % nc),
                marks["scatter"] + q * nx + x,
            )

        def stays(m, q):
            return (m * nc + core == x) & (mine_f[q] % nc == core)

        def scatter_step(q):
            for m in range(pairs_x):
                pairs[m, q].wait_recv()
                value = blocks[m * nc + core, q].astype(F32) + pair[m, q].astype(F32)
                value = value.astype(BF16).reshape(SUB, part, lanes)

                @pl.when(stays(m, q))
                def _():
                    line[mine_f[q] // nc] = value

                @pl.when(jnp.logical_not(stays(m, q)))
                def _():
                    scatter_out[m, q] = value
                    scatter_copy(m, q).start()

        middle = nz // 2
        low_half = zl < middle

        def chain_copy(kind, d, s, there):
            return remote(
                chain_out.at[d, s],
                chain_in.at[kind, d, s],
                marks["chain"] + d * SUB + s,
                device(zl=there),
                marks["chain"] + (kind * nz + d) * SUB + s,
            )

        def chain_place(d):
            same = low_half if d < middle else jnp.logical_not(low_half)
            first, end = (0, middle - 1) if d < middle else (middle, nz - 1)
            up = zl < d
            kind = jnp.where(same, jnp.where(up, 0, 1), 2)
            edge = jnp.where(low_half, middle - 1, middle)
            beside = jnp.where(up, zl + 1, zl - 1)
            there = jnp.where(jnp.logical_not(same) & (zl == edge), d, beside)
            starts = jnp.where(
                same,
                jnp.where(up, zl == first, zl == end),
                jnp.where(low_half, zl == 0, zl == nz - 1),
            )
            return kind, there, starts

        def chain_step(q, s_x):
            f = nq * s_x + q
            d = f // nc
            kind, there, starts = chain_place(d)

            @pl.when(core == f % nc)
            def _():
                @pl.when(jnp.logical_not((x == s_x) & (core == x % nc)))
                def _():
                    remote(
                        scatter_out.at[0, q],
                        line.at[d],
                        marks["scatter"],
                        device(core=1 - core),
                        marks["scatter"] + q * nx + s_x,
                    ).wait_recv()

                @pl.when(zl != d)
                def _():
                    for s in range(SUB):

                        @pl.when(starts)
                        def _():
                            chain_out[d, s] = line[d, s]

                        @pl.when(jnp.logical_not(starts))
                        def _():
                            chain_copy(kind, d, s, there).wait_recv()
                            chain_out[d, s] = (
                                line[d, s].astype(F32)
                                + chain_in[kind, d, s].astype(F32)
                            ).astype(BF16)

                        chain_copy(kind, d, s, there).start()

        tasks = []

        def at(time, what, *which):
            tasks.append((time, len(tasks), what, which))

        gap = 3.7
        for q in range(nq):
            now = q * gap
            at(now, pass_z, q)
            at(now + 2.0, pass_core, q)
            at(now + 4.0, make_tile, q)
            at(now + 9.0, sum_step, q)
            at(now + 13.0, swap_step, q)
            at(now + 20.5, grad_step, q)
            at(now + 24.5, gather_step, q)
            at(now + 28.5, back_step, q)
            now += 28.5 + (4.0 if q < nq - 1 else 2.0)
            at(now, scatter_step, q)
            if q == nq - 1:
                at(now, close_a)
            for s_x in range(nx):
                at(now + 5.0, chain_step, q, s_x)
        for _, _, what, which in sorted(tasks, key=lambda task: task[:2]):
            what(*which)

        total_a = acc_a[x]
        for k in range(1, nx):
            backs[k].wait_recv()
            total_a = total_a + recv_a[k].astype(F32)
        out_a[...] = total_a.astype(BF16)

        here = jnp.where(low_half, zl, zl - middle)
        beside_me = (zl + 1) % nz
        for s in range(SUB):
            owned_b[...] = line[zl, s].astype(F32)
            chain_copy(2, zl, s, beside_me).wait_recv()
            owned_b[...] += chain_in[2, zl, s].astype(F32)

            @pl.when(here > 0)
            def _():
                chain_copy(0, zl, s, beside_me).wait_recv()
                owned_b[...] += chain_in[0, zl, s].astype(F32)

            @pl.when(here < middle - 1)
            def _():
                chain_copy(1, zl, s, beside_me).wait_recv()
                owned_b[...] += chain_in[1, zl, s].astype(F32)

            out_b[s * part : (s + 1) * part] = owned_b[...].astype(BF16)

        for q in range(nq):
            for m in range(pairs_x):

                @pl.when(jnp.logical_not(stays(m, q)))
                def _():
                    scatter_copy(m, q).wait_send()

        for d in range(nz):

            @pl.when(zl != d)
            def _():
                kind, there, _ = chain_place(d)
                for s in range(SUB):
                    chain_copy(kind, d, s, there).wait_send()

        for copy in waiting:
            copy.wait_send()

    vmem = pltpu.VMEM
    count = nq + 1
    shapes = [
        vmem((nx, rows, lanes), BF16),
        vmem((nq, nx, rows, lanes), BF16),
        vmem((nx, nq, rows, lanes), BF16),
        vmem((nx, rows, lanes), BF16),
        vmem((nq, nx, rows, lanes), BF16),
        vmem((lanes, nx * rows), BF16),
        vmem((2, nx, 2 * count, lanes), F32),
        vmem((ny, 2 * count, lanes), F32),
        vmem((2, 2 * count, lanes), F32),
        vmem((2 * count, lanes), F32),
        vmem((nq, ny, slot, lanes), BF16),
        vmem((len(routes), nq, slot, lanes), BF16),
        vmem((len(routes), nq, slot, lanes), BF16),
        vmem((len(routes), nq, slot, lanes), BF16),
        vmem((nq, slot, lanes), F32),
        vmem((nq, slot, lanes), BF16),
        vmem((nq, slot, lanes), BF16),
        vmem((nq, ny, slot, lanes), BF16),
        vmem((nx, rows, lanes), F32),
        vmem((nx, rows, lanes), BF16),
        vmem((nx, rows, lanes), BF16),
        vmem((nx, nq, rows, lanes), BF16),
        vmem((nx // nc, nq, rows, lanes), BF16),
        vmem((pairs_x, nq, SUB, part, lanes), BF16),
        vmem((nz, SUB, part, lanes), BF16),
        vmem((3, nz, SUB, part, lanes), BF16),
        vmem((nz, SUB, part, lanes), BF16),
        vmem((part, lanes), F32),
        pltpu.SemaphoreType.DMA((copies.count,)),
        pltpu.SemaphoreType.DMA((copies.count,)),
        pltpu.SemaphoreType.DMA((nq,)),
    ]
    result = jax.ShapeDtypeStruct((rows, lanes), BF16)
    return pl.pallas_call(
        kernel,
        out_shape=(result, result),
        in_specs=[pl.BlockSpec(memory_space=vmem)] * 2,
        out_specs=(pl.BlockSpec(memory_space=vmem),) * 2,
        scratch_shapes=shapes,
        compiler_params=pltpu.CompilerParams(
            collective_id=0, has_side_effects=True, vmem_limit_bytes=56 << 20
        ),
    )


def solution(mesh):
    def local(z_a, z_b):
        grad_a, grad_b = build(Plan(mesh, *z_a.shape))(z_a, z_b)
        block = z_a.shape[1]
        return grad_a[:, :block], grad_b[:, :block]

    return jax.shard_map(
        local,
        mesh=mesh,
        in_specs=(P("dp", "fsdp"), P("dp", None)),
        out_specs=(P("dp", "fsdp"), P("dp", "fsdp")),
        check_vma=False,
    )
```

```python
import jax
import jax.numpy as jnp
from jax import lax
from jax.experimental import pallas as pl
from jax.experimental.pallas import tpu as pltpu
from jax.sharding import PartitionSpec as P

EPS = 1e-05
WEIGHT = 0.0051
LANES = 128
CORES = 2
Z_HI = 2
X_CHIPS = 4
SUB = 4
MESH = pl.DeviceIdType.MESH
F32 = jnp.float32
BF16 = jnp.bfloat16


class Plan:
    def __init__(self, mesh, rows, block):
        fsdp, dp = mesh.shape["fsdp"], mesh.shape["dp"]
        self.nx, self.nh, self.nc = X_CHIPS, Z_HI, CORES
        self.ny = dp // (self.nx * self.nh)
        self.nz = fsdp // self.nc
        self.nf = fsdp
        self.nq = self.nf // self.nx
        self.rows, self.block = rows, block
        self.lanes = -(-(block + 1) // LANES) * LANES
        self.slot = self.lanes // self.ny
        self.batch = rows * dp
        right = self.ny // 2
        self.routes = []
        for step, reach in ((1, right), (-1, self.ny - 1 - right)):
            for near in range(1, reach + 1, 2):
                self.routes.append((step, near, near < reach))


class Copies:
    def __init__(self):
        self.count = 0

    def take(self, n=1):
        first = self.count
        self.count += n
        return first


def build(p):
    copies = Copies()
    nx, ny, nh, nz, nc, nq = p.nx, p.ny, p.nh, p.nz, p.nc, p.nq
    rows, lanes, slot, block = p.rows, p.lanes, p.slot, p.block
    half = rows // nc
    quarter = half // 2
    part = rows // SUB
    routes = p.routes
    pairs_x = nx // nc
    marks = dict(
        a=copies.take(nx),
        b=copies.take(nx * nq),
        pass_z=copies.take(nx * nq),
        pass_c=copies.take(nx * nq),
        stat_x=copies.take(nx),
        stat_y=copies.take(ny),
        stat_h=copies.take(1),
        low_y=copies.take(ny),
        low_h=copies.take(1),
        mid=copies.take(len(routes) * nq),
        fin=copies.take(len(routes) * nq),
        swap=copies.take(nq),
        near=copies.take(len(routes) * nq),
        far=copies.take(len(routes) * nq),
        pair=copies.take(pairs_x * nq),
        back_a=copies.take(nx),
        scatter=copies.take(max(pairs_x, nx) * nq),
        chain=copies.take(3 * nz * SUB),
    )

    def kernel(
        za,
        zb,
        out,
        raw_a,
        raw_b,
        pack,
        low_a,
        low_b,
        low_t,
        stat_x,
        stat_y,
        stat_h,
        low_sum,
        low_pair,
        half_low,
        group,
        mean,
        shift_b,
        column,
        tile,
        mid_in,
        mid_out,
        fin_in,
        owned,
        swap_out,
        swap_in,
        grad,
        acc_a,
        send_a,
        recv_a,
        blocks,
        pair,
        scatter_out,
        line,
        chain_in,
        chain_out,
        owned_b,
        send_sem,
        recv_sem,
        own_sem,
    ):
        dp = lax.axis_index("dp")
        fs = lax.axis_index("fsdp")
        x = dp % nx
        h = (dp // nx) % nh
        y = dp // (nx * nh)
        core = fs % nc
        zl = fs // nc

        def device(x=x, y=y, h=h, zl=zl, core=core):
            return {"dp": (y * nh + h) * nx + x, "fsdp": zl * nc + core}

        def remote(src, dst, mark, there, recv_mark=None):
            arrived = mark if recv_mark is None else recv_mark
            return pltpu.make_async_remote_copy(
                src_ref=src,
                dst_ref=dst,
                send_sem=send_sem.at[mark],
                recv_sem=recv_sem.at[arrived],
                device_id=there,
                device_id_type=MESH,
            )

        barrier = pltpu.get_barrier_semaphore()

        def greet(there):
            pl.semaphore_signal(barrier, inc=1, device_id=there, device_id_type=MESH)

        greet(device(core=1 - core))
        for k in range(1, nx):
            greet(device(x=(x + k) % nx))
            greet(device(x=(x + k) % nx, core=1 - core))
        for k in range(1, ny):
            greet(device(y=(y + k) % ny))
        greet(device(h=1 - h))
        for k in range(1, nz):
            greet(device(zl=(zl + k) % nz))

        waiting = []

        zero = jnp.zeros((rows, lanes - block), BF16)
        raw_a[x] = jnp.concatenate([za[...], zero], axis=1)
        for f in range(p.nf):
            piece = zb[:, f * block : (f + 1) * block]
            pack[f // nq, f % nq] = jnp.concatenate([piece, zero], axis=1)

        def sums(value):
            v = value.astype(F32)
            return (
                jnp.sum(v, axis=0, keepdims=True),
                jnp.sum(v * v, axis=0, keepdims=True),
            )

        first = [sums(pack[f // nq, f % nq]) for f in range(p.nf)]
        first_a = sums(raw_a[x])
        for t in range(nx):
            both = first[t * nq : (t + 1) * nq] + [first_a]
            stat_x[0, t] = jnp.concatenate(
                [s for s, _ in both] + [s for _, s in both], axis=0
            )

        pl.semaphore_wait(barrier, 2 * (nx - 1) + ny - 1 + nz - 1 + 2)

        def start(copy):
            copy.start()
            waiting.append(copy)
            return copy

        got_x, got_y = {}, {}
        for k in range(1, nx):
            t = (x + k) % nx
            got_x[k] = start(
                remote(
                    stat_x.at[0, t],
                    stat_x.at[1, k],
                    marks["stat_x"] + k,
                    device(x=t),
                )
            )
        into_a = {}
        for k in range(1, nx):
            into_a[k] = start(
                remote(
                    raw_a.at[x], raw_a.at[x], marks["a"] + k, device(x=(x + k) % nx)
                )
            )
        own_rows = pl.ds(core * half + (zl % 2) * quarter, quarter)
        core_rows = pl.ds(core * half, half)
        z_pair = device(zl=zl + 1 - 2 * (zl % 2))
        into_b = {}
        for q in range(nq):
            for k in range(1, nx):
                t = (x + k) % nx
                into_b[q, k] = start(
                    remote(
                        pack.at[t, q, own_rows],
                        raw_b.at[q, x, own_rows],
                        marks["b"] + q * nx + k,
                        device(x=t),
                    )
                )
        mine = []
        for q in range(nq):
            copy = pltpu.make_async_copy(pack.at[x, q], raw_b.at[q, x], own_sem.at[q])
            copy.start()
            mine.append(copy)

        total = stat_x[0, x]
        for k in range(1, nx):
            got_x[k].wait_recv()
            total = total + stat_x[1, k]
        stat_y[0] = total
        for k in range(1, ny):
            got_y[k] = start(
                remote(
                    stat_y.at[0],
                    stat_y.at[k],
                    marks["stat_y"] + k,
                    device(y=(y + k) % ny),
                )
            )
        count = nq + 1
        images = nx * rows
        group[:count] = total[:count] / images
        low_pair[0] = jnp.zeros((8, lanes), F32)
        got_h, got_low = {}, {}

        def half_moments():
            total = stat_y[0]
            for k in range(1, ny):
                got_y[k].wait_recv()
                total = total + stat_y[k]
            stat_h[0] = total
            got_h[0] = start(
                remote(stat_h.at[0], stat_h.at[1], marks["stat_h"], device(h=1 - h))
            )

        def all_moments():
            got_h[0].wait_recv()
            ours, theirs = stat_h[0], stat_h[1]
            total = (ours + theirs) / p.batch
            center = total[:count]
            inverse = lax.rsqrt(total[count:] - center * center + EPS)
            mean[:count] = center
            mean[count:] = inverse
            half_mean = ours[:count] / (images * ny)
            apart = half_mean - theirs[:count] / (images * ny)
            shifts = [stat_y[k][:count] / images - half_mean for k in range(ny)]
            fill = [jnp.zeros((16 - ny - 2, lanes), F32)] if ny < 14 else []
            for q in range(count):
                table = jnp.concatenate(
                    [v[q : q + 1] for v in shifts]
                    + [apart[q : q + 1], inverse[q : q + 1]]
                    + fill,
                    axis=0,
                )
                if q < nq:
                    shift_b[q] = table
                else:
                    column[...] = jnp.transpose(table)

        lane = lax.broadcasted_iota(jnp.int32, (rows, lanes), 1)

        def normal(raw, which):
            v = raw.astype(F32)
            return (v - mean[which : which + 1, :]) * mean[
                count + which : count + which + 1, :
            ]

        def centred(raw, which):
            return raw.astype(F32) - group[which : which + 1, :]

        def center_a():
            for k in range(1, nx):
                into_a[k].wait_recv()
            for i in range(nx):
                low_t[:, i * rows : (i + 1) * rows] = jnp.transpose(
                    centred(raw_a[i], nq)
                ).astype(BF16)

        def normalise(which):
            def low_step(i, _):
                if which < nq:
                    value = normal(raw_b[which, i], which).astype(BF16)
                    low_b[which, i] = value
                else:
                    value = normal(raw_a[i], which).astype(BF16)
                    low_a[i] = value
                low_pair[0, which : which + 1] += jnp.sum(
                    value.astype(F32), axis=0, keepdims=True
                )
                return 0

            lax.fori_loop(0, nx, low_step, 0)

        def low_over_y():
            low_sum[0] = low_pair[0]
            for k in range(1, ny):
                got_low[k] = start(
                    remote(
                        low_sum.at[0],
                        low_sum.at[k],
                        marks["low_y"] + k,
                        device(y=(y + k) % ny),
                    )
                )

        def low_over_h():
            total = low_sum[0]
            for k in range(1, ny):
                got_low[k].wait_recv()
                total = total + low_sum[k]
            half_low[...] = total
            got_low[0] = start(
                remote(half_low, low_pair.at[1], marks["low_h"], device(h=1 - h))
            )

        low_mean = {}

        def low_means():
            got_low[0].wait_recv()
            value = (half_low[...] + low_pair[1]) / p.batch
            low_mean["row"] = value
            low_mean["column"] = jnp.transpose(value)[:, nq : nq + 1]

        passed_z, passed, swaps, pairs = {}, {}, {}, {}
        mid, fin, near_ag, far_ag = {}, {}, {}, {}

        def pass_z(q):
            for k in range(1, nx):
                into_b[q, k].wait_recv()
                s = (x + nx - k) % nx
                passed_z[q, k] = start(
                    remote(
                        raw_b.at[q, s, own_rows],
                        raw_b.at[q, s, own_rows],
                        marks["pass_z"] + q * nx + k,
                        z_pair,
                    )
                )

        def pass_core(q):
            for k in range(1, nx):
                passed_z[q, k].wait_recv()
                s = (x + nx - k) % nx
                passed[q, k] = start(
                    remote(
                        raw_b.at[q, s, core_rows],
                        raw_b.at[q, s, core_rows],
                        marks["pass_c"] + q * nx + k,
                        device(core=1 - core),
                    )
                )

        flip = 1 - 2 * (core % 2)

        def along(distance):
            return (y + flip * distance + ny) % ny

        def make_tile(q):
            mine[q].wait()
            for k in range(1, nx):
                passed[q, k].wait_recv()

            def low_b_step(i, _):
                low_b[q, i] = centred(raw_b[q, i], q).astype(BF16)
                return 0

            lax.fori_loop(0, nx, low_b_step, 0)
            product = jnp.dot(
                low_t[...],
                low_b[q].reshape(nx * rows, lanes),
                preferred_element_type=F32,
            )
            tile[q] = product.astype(BF16).reshape(ny, slot, lanes)
            for r, (step, near, goes_on) in enumerate(routes):
                mark = r * nq + q
                if goes_on:
                    t = along(step * (near + 1))
                    mid[r, q] = start(
                        remote(
                            tile.at[q, t],
                            mid_in.at[r, q],
                            marks["mid"] + mark,
                            device(y=along(step)),
                        )
                    )
                else:
                    t = along(step * near)
                    fin[r, q] = start(
                        remote(
                            tile.at[q, t],
                            fin_in.at[r, q],
                            marks["fin"] + mark,
                            device(y=t),
                        )
                    )

        def sum_step(q):
            for r, (step, near, goes_on) in enumerate(routes):
                if goes_on:
                    t = along(step * near)
                    mid[r, q].wait_recv()
                    mid_out[r, q] = (
                        mid_in[r, q].astype(F32) + tile[q, t].astype(F32)
                    ).astype(BF16)
                    fin[r, q] = start(
                        remote(
                            mid_out.at[r, q],
                            fin_in.at[r, q],
                            marks["fin"] + r * nq + q,
                            device(y=t),
                        )
                    )

        own_slot = pl.ds(pl.multiple_of(y * slot, 8), slot)

        def swap_step(q):
            value = tile[q, y].astype(F32)
            for r in range(len(routes)):
                fin[r, q].wait_recv()
                value = value + fin_in[r, q].astype(F32)
            spread = jnp.zeros((slot, lanes), F32)
            for k in range(ny):
                spread += column[own_slot, k : k + 1] * shift_b[q, k : k + 1]
            value = value + images * spread
            owned[q] = value
            swap_out[q] = value.astype(BF16)
            swaps[q] = start(
                remote(
                    swap_out.at[q], swap_in.at[q], marks["swap"] + q, device(h=1 - h)
                )
            )

        def grad_step(q):
            swaps[q].wait_recv()
            spread = column[own_slot, ny : ny + 1] * shift_b[q, ny : ny + 1]
            corr = owned[q] + swap_in[q].astype(F32) + (p.batch / 4) * spread
            scale = column[own_slot, ny + 1 : ny + 2] * shift_b[q, ny + 1 : ny + 2]
            corr = corr * scale / p.batch
            row = y * slot + lax.broadcasted_iota(jnp.int32, (slot, lanes), 0)
            col = lax.broadcasted_iota(jnp.int32, (slot, lanes), 1)
            on = (row == col) & (fs == nq * x + q)
            grad[q, y] = jnp.where(
                on, -2.0 * (1.0 - corr), 2.0 * WEIGHT * corr
            ).astype(BF16)
            for r, (step, near, goes_on) in enumerate(routes):
                near_ag[r, q] = start(
                    remote(
                        grad.at[q, y],
                        grad.at[q, y],
                        marks["near"] + r * nq + q,
                        device(y=along(step * near)),
                    )
                )

        def gather_step(q):
            for r, (step, near, goes_on) in enumerate(routes):
                near_ag[r, q].wait_recv()
                if goes_on:
                    t = along(-step * near)
                    far_ag[r, q] = start(
                        remote(
                            grad.at[q, t],
                            grad.at[q, t],
                            marks["far"] + r * nq + q,
                            device(y=along(step)),
                        )
                    )

        means_a = [jnp.zeros((1, lanes), F32), jnp.zeros((1, lanes), F32)]

        def back_step(q):
            for r, (step, near, goes_on) in enumerate(routes):
                if goes_on:
                    far_ag[r, q].wait_recv()
            row = lax.broadcasted_iota(jnp.int32, (lanes, lanes), 0)
            col = lax.broadcasted_iota(jnp.int32, (lanes, lanes), 1)
            g = grad[q].reshape(lanes, lanes).astype(F32)
            mean_b = low_mean["row"][q : q + 1]
            mean_a = low_mean["column"]
            g = jnp.where((row < block) & (col < block), g, 0.0)
            on = (row == col) & (fs == nq * x + q)
            cross = g * jnp.where(on, 1.0 + 0.5 * g, g / (2.0 * WEIGHT))
            flat_b = jnp.sum(g * mean_a, axis=0, keepdims=True)
            cross_b = jnp.sum(cross, axis=0, keepdims=True)
            low_g = g.astype(BF16)

            def back_b_step(i, _):
                value = jnp.dot(low_a[i], low_g, preferred_element_type=F32)
                value = value - flat_b - normal(raw_b[q, i], q) * cross_b
                blocks[i, q] = (value * mean[count + q : count + q + 1, :]).astype(BF16)
                return 0

            lax.fori_loop(0, nx, back_b_step, 0)
            for m in range(nx // nc):
                pairs[m, q] = start(
                    remote(
                        blocks.at[m * nc + 1 - core, q],
                        pair.at[m, q],
                        marks["pair"] + m * nq + q,
                        device(core=1 - core),
                    )
                )

            means_a[0] += jnp.sum(jnp.transpose(g * mean_b), axis=0, keepdims=True)
            means_a[1] += jnp.sum(jnp.transpose(cross), axis=0, keepdims=True)

            def back_a_step(i, _):
                value = lax.dot_general(
                    low_b[q, i],
                    low_g,
                    (((1,), (1,)), ((), ())),
                    preferred_element_type=F32,
                )
                acc_a[i] = value if q == 0 else acc_a[i] + value
                return 0

            lax.fori_loop(0, nx, back_a_step, 0)

        backs = {}

        def close_a():
            inv_a = mean[count + nq : count + nq + 1, :]

            def close_a_step(i, _):
                value = acc_a[i] - means_a[0] - normal(raw_a[i], nq) * means_a[1]
                value = value * inv_a
                acc_a[i] = value
                send_a[i] = value.astype(BF16)
                return 0

            lax.fori_loop(0, nx, close_a_step, 0)
            for k in range(1, nx):
                t = (x + k) % nx
                backs[k] = start(
                    remote(
                        send_a.at[t], recv_a.at[k], marks["back_a"] + k, device(x=t)
                    )
                )

        mine_f = [nq * x + q for q in range(nq)]

        def scatter_copy(m, q):
            return remote(
                scatter_out.at[m, q],
                line.at[mine_f[q] // nc],
                marks["scatter"] + q * pairs_x + m,
                device(x=m * nc + core, core=mine_f[q] % nc),
                marks["scatter"] + q * nx + x,
            )

        def stays(m, q):
            return (m * nc + core == x) & (mine_f[q] % nc == core)

        def scatter_step(q):
            for m in range(pairs_x):
                pairs[m, q].wait_recv()
                value = blocks[m * nc + core, q].astype(F32) + pair[m, q].astype(F32)
                value = value.astype(BF16).reshape(SUB, part, lanes)

                @pl.when(stays(m, q))
                def _():
                    line[mine_f[q] // nc] = value

                @pl.when(jnp.logical_not(stays(m, q)))
                def _():
                    scatter_out[m, q] = value
                    scatter_copy(m, q).start()

        middle = nz // 2
        low_half = zl < middle

        def chain_copy(kind, d, s, there):
            return remote(
                chain_out.at[d, s],
                chain_in.at[kind, d, s],
                marks["chain"] + d * SUB + s,
                device(zl=there),
                marks["chain"] + (kind * nz + d) * SUB + s,
            )

        def chain_place(d):
            same = low_half if d < middle else jnp.logical_not(low_half)
            first, end = (0, middle - 1) if d < middle else (middle, nz - 1)
            up = zl < d
            kind = jnp.where(same, jnp.where(up, 0, 1), 2)
            edge = jnp.where(low_half, middle - 1, middle)
            beside = jnp.where(up, zl + 1, zl - 1)
            there = jnp.where(jnp.logical_not(same) & (zl == edge), d, beside)
            level = jnp.where(
                same,
                jnp.where(up, zl - first, end - zl),
                jnp.where(low_half, zl, nz - 1 - zl),
            )
            return kind, there, level

        def chain_step(q, s_x, at_level):
            f = nq * s_x + q
            d = f // nc
            kind, there, level = chain_place(d)

            if at_level == 0:

                @pl.when(
                    (core == f % nc)
                    & jnp.logical_not((x == s_x) & (core == x % nc))
                )
                def _():
                    remote(
                        scatter_out.at[0, q],
                        line.at[d],
                        marks["scatter"],
                        device(core=1 - core),
                        marks["scatter"] + q * nx + s_x,
                    ).wait_recv()

            @pl.when((core == f % nc) & (zl != d) & (level == at_level))
            def _():
                for s in range(SUB):
                    if at_level == 0:
                        chain_out[d, s] = line[d, s]
                    else:
                        chain_copy(kind, d, s, there).wait_recv()
                        chain_out[d, s] = (
                            line[d, s].astype(F32) + chain_in[kind, d, s].astype(F32)
                        ).astype(BF16)
                    chain_copy(kind, d, s, there).start()

        tasks = []

        def at(time, what, *which):
            tasks.append((time, len(tasks), what, which))

        at(7.5, center_a)
        at(12.6, half_moments)
        at(20.2, all_moments)
        at(22.8, normalise, nq)
        at(27.5, low_over_y)
        at(35.5, low_over_h)
        at(43.5, low_means)
        for q in range(nq):
            at(11.0 + 2.3 * q, pass_z, q)
            at(14.0 + 2.8 * q, pass_core, q)
            at(16.0 + 2.8 * q, make_tile, q)
            at(23.0 + 1.8 * q, normalise, q)
            now = 21.0 + 3.7 * q
            at(now, sum_step, q)
            at(now + 5.5, swap_step, q)
            at(now + 13.5, grad_step, q)
            at(now + 19.0, gather_step, q)
            now += 23.0
            at(now, back_step, q)
            now += 4.0 if q < nq - 1 else 2.0
            at(now, scatter_step, q)
            if q == nq - 1:
                at(now, close_a)
            for level in range(middle):
                for s_x in range(nx):
                    at(now + 4.5 + 3.0 * level, chain_step, q, s_x, level)
        for _, _, what, which in sorted(tasks, key=lambda task: task[:2]):
            what(*which)

        total_a = acc_a[x]
        for k in range(1, nx):
            backs[k].wait_recv()
            total_a = total_a + recv_a[k].astype(F32)
        out[0] = total_a

        here = jnp.where(low_half, zl, zl - middle)
        beside_me = (zl + 1) % nz
        for s in range(SUB):
            owned_b[...] = line[zl, s].astype(F32)
            chain_copy(2, zl, s, beside_me).wait_recv()
            owned_b[...] += chain_in[2, zl, s].astype(F32)

            @pl.when(here > 0)
            def _():
                chain_copy(0, zl, s, beside_me).wait_recv()
                owned_b[...] += chain_in[0, zl, s].astype(F32)

            @pl.when(here < middle - 1)
            def _():
                chain_copy(1, zl, s, beside_me).wait_recv()
                owned_b[...] += chain_in[1, zl, s].astype(F32)

            out[1, s * part : (s + 1) * part] = owned_b[...]

        for q in range(nq):
            for m in range(pairs_x):

                @pl.when(jnp.logical_not(stays(m, q)))
                def _():
                    scatter_copy(m, q).wait_send()

        for d in range(nz):

            @pl.when(zl != d)
            def _():
                kind, there, _ = chain_place(d)
                for s in range(SUB):
                    chain_copy(kind, d, s, there).wait_send()

        for copy in waiting:
            copy.wait_send()

    vmem = pltpu.VMEM
    count = nq + 1
    shapes = [
        vmem((nx, rows, lanes), BF16),
        vmem((nq, nx, rows, lanes), BF16),
        vmem((nx, nq, rows, lanes), BF16),
        vmem((nx, rows, lanes), BF16),
        vmem((nq, nx, rows, lanes), BF16),
        vmem((lanes, nx * rows), BF16),
        vmem((2, nx, 2 * count, lanes), F32),
        vmem((ny, 2 * count, lanes), F32),
        vmem((2, 2 * count, lanes), F32),
        vmem((ny, 8, lanes), F32),
        vmem((2, 8, lanes), F32),
        vmem((8, lanes), F32),
        vmem((8, lanes), F32),
        vmem((2 * count, lanes), F32),
        vmem((nq, 16, lanes), F32),
        vmem((lanes, 16), F32),
        vmem((nq, ny, slot, lanes), BF16),
        vmem((len(routes), nq, slot, lanes), BF16),
        vmem((len(routes), nq, slot, lanes), BF16),
        vmem((len(routes), nq, slot, lanes), BF16),
        vmem((nq, slot, lanes), F32),
        vmem((nq, slot, lanes), BF16),
        vmem((nq, slot, lanes), BF16),
        vmem((nq, ny, slot, lanes), BF16),
        vmem((nx, rows, lanes), F32),
        vmem((nx, rows, lanes), BF16),
        vmem((nx, rows, lanes), BF16),
        vmem((nx, nq, rows, lanes), BF16),
        vmem((nx // nc, nq, rows, lanes), BF16),
        vmem((pairs_x, nq, SUB, part, lanes), BF16),
        vmem((nz, SUB, part, lanes), BF16),
        vmem((3, nz, SUB, part, lanes), BF16),
        vmem((nz, SUB, part, lanes), BF16),
        vmem((part, lanes), F32),
        pltpu.SemaphoreType.DMA((copies.count,)),
        pltpu.SemaphoreType.DMA((copies.count,)),
        pltpu.SemaphoreType.DMA((nq,)),
    ]
    result = jax.ShapeDtypeStruct((2, rows, lanes), F32)
    return pl.pallas_call(
        kernel,
        out_shape=result,
        in_specs=[pl.BlockSpec(memory_space=vmem)] * 2,
        out_specs=pl.BlockSpec(memory_space=vmem),
        scratch_shapes=shapes,
        compiler_params=pltpu.CompilerParams(
            collective_id=0, has_side_effects=True, vmem_limit_bytes=56 << 20
        ),
    )


def solution(mesh):
    def local(z_a, z_b):
        grads = build(Plan(mesh, *z_a.shape))(z_a, z_b)
        block = z_a.shape[1]
        return grads[0, :, :block].astype(BF16), grads[1, :, :block].astype(BF16)

    return jax.shard_map(
        local,
        mesh=mesh,
        in_specs=(P("dp", "fsdp"), P("dp", None)),
        out_specs=(P("dp", "fsdp"), P("dp", "fsdp")),
        check_vma=False,
    )
```

```python
import jax
import jax.numpy as jnp
from jax import lax
from jax.experimental import pallas as pl
from jax.experimental.pallas import tpu as pltpu
from jax.sharding import PartitionSpec as P

EPS = 1e-05
WEIGHT = 0.0051
LANES = 128
CORES = 2
Z_HI = 2
X_CHIPS = 4
SUB = 4
MESH = pl.DeviceIdType.MESH
F32 = jnp.float32
BF16 = jnp.bfloat16


class Plan:
    def __init__(self, mesh, rows, block):
        fsdp, dp = mesh.shape["fsdp"], mesh.shape["dp"]
        self.nx, self.nh, self.nc = X_CHIPS, Z_HI, CORES
        self.ny = dp // (self.nx * self.nh)
        self.nz = fsdp // self.nc
        self.nf = fsdp
        self.nq = self.nf // self.nx
        self.rows, self.block = rows, block
        self.lanes = -(-(block + 1) // LANES) * LANES
        self.slot = self.lanes // self.ny
        self.batch = rows * dp
        right = self.ny // 2
        self.routes = []
        for step, reach in ((1, right), (-1, self.ny - 1 - right)):
            for near in range(1, reach + 1, 2):
                self.routes.append((step, near, near < reach))


class Copies:
    def __init__(self):
        self.count = 0

    def take(self, n=1):
        first = self.count
        self.count += n
        return first


def build(p):
    copies = Copies()
    nx, ny, nh, nz, nc, nq = p.nx, p.ny, p.nh, p.nz, p.nc, p.nq
    rows, lanes, slot, block = p.rows, p.lanes, p.slot, p.block
    half = rows // nc
    quarter = half // 2
    part = rows // SUB
    routes = p.routes
    pairs_x = nx // nc
    marks = dict(
        a=copies.take(nx),
        b=copies.take(nx * nq),
        pass_z=copies.take(nx * nq),
        pass_c=copies.take(nx * nq),
        stat_x=copies.take(nx),
        stat_y=copies.take(ny),
        stat_h=copies.take(1),
        low_y=copies.take(ny),
        low_h=copies.take(1),
        mid=copies.take(len(routes) * nq),
        fin=copies.take(len(routes) * nq),
        swap=copies.take(nq),
        near=copies.take(len(routes) * nq),
        far=copies.take(len(routes) * nq),
        pair=copies.take(pairs_x * nq),
        back_a=copies.take(nx),
        scatter=copies.take(max(pairs_x, nx) * nq),
        chain=copies.take(3 * nz * SUB),
    )

    def kernel(
        za,
        zb,
        out,
        raw_a,
        raw_b,
        pack,
        low_a,
        low_b,
        low_t,
        stat_x,
        stat_y,
        stat_h,
        low_sum,
        low_pair,
        half_low,
        group,
        mean,
        shift_b,
        column,
        tile,
        mid_in,
        mid_out,
        fin_in,
        owned,
        swap_out,
        swap_in,
        grad,
        acc_a,
        send_a,
        recv_a,
        blocks,
        pair,
        scatter_out,
        line,
        chain_in,
        chain_out,
        owned_b,
        send_sem,
        recv_sem,
        own_sem,
    ):
        dp = lax.axis_index("dp")
        fs = lax.axis_index("fsdp")
        x = dp % nx
        h = (dp // nx) % nh
        y = dp // (nx * nh)
        core = fs % nc
        zl = fs // nc

        def device(x=x, y=y, h=h, zl=zl, core=core):
            return {"dp": (y * nh + h) * nx + x, "fsdp": zl * nc + core}

        def remote(src, dst, mark, there, recv_mark=None):
            arrived = mark if recv_mark is None else recv_mark
            return pltpu.make_async_remote_copy(
                src_ref=src,
                dst_ref=dst,
                send_sem=send_sem.at[mark],
                recv_sem=recv_sem.at[arrived],
                device_id=there,
                device_id_type=MESH,
            )

        barrier = pltpu.get_barrier_semaphore()

        def greet(there):
            pl.semaphore_signal(barrier, inc=1, device_id=there, device_id_type=MESH)

        greet(device(core=1 - core))
        for k in range(1, nx):
            greet(device(x=(x + k) % nx))
            greet(device(x=(x + k) % nx, core=1 - core))
        for k in range(1, ny):
            greet(device(y=(y + k) % ny))
        greet(device(h=1 - h))
        for k in range(1, nz):
            greet(device(zl=(zl + k) % nz))

        waiting = []

        zero = jnp.zeros((rows, lanes - block), BF16)
        raw_a[x] = jnp.concatenate([za[...], zero], axis=1)
        for f in range(p.nf):
            piece = zb[:, f * block : (f + 1) * block]
            pack[f // nq, f % nq] = jnp.concatenate([piece, zero], axis=1)

        def sums(value):
            v = value.astype(F32)
            return (
                jnp.sum(v, axis=0, keepdims=True),
                jnp.sum(v * v, axis=0, keepdims=True),
            )

        first = [sums(pack[f // nq, f % nq]) for f in range(p.nf)]
        first_a = sums(raw_a[x])
        for t in range(nx):
            both = first[t * nq : (t + 1) * nq] + [first_a]
            stat_x[0, t] = jnp.concatenate(
                [s for s, _ in both] + [s for _, s in both], axis=0
            )

        pl.semaphore_wait(barrier, 2 * (nx - 1) + ny - 1 + nz - 1 + 2)

        def start(copy):
            copy.start()
            waiting.append(copy)
            return copy

        got_x, got_y = {}, {}
        for k in range(1, nx):
            t = (x + k) % nx
            got_x[k] = start(
                remote(
                    stat_x.at[0, t],
                    stat_x.at[1, k],
                    marks["stat_x"] + k,
                    device(x=t),
                )
            )
        into_a = {}
        for k in range(1, nx):
            into_a[k] = start(
                remote(
                    raw_a.at[x], raw_a.at[x], marks["a"] + k, device(x=(x + k) % nx)
                )
            )
        own_rows = pl.ds(core * half, half)
        core_rows = pl.ds(core * half, half)
        z_pair = device(zl=zl + 1 - 2 * (zl % 2))
        into_b = {}
        for q in range(nq):
            for k in range(1, nx):
                t = (x + k) % nx
                into_b[q, k] = start(
                    remote(
                        pack.at[t, q, own_rows],
                        raw_b.at[q, x, own_rows],
                        marks["b"] + q * nx + k,
                        device(x=t),
                    )
                )
        mine = []
        for q in range(nq):
            copy = pltpu.make_async_copy(pack.at[x, q], raw_b.at[q, x], own_sem.at[q])
            copy.start()
            mine.append(copy)

        total = stat_x[0, x]
        for k in range(1, nx):
            got_x[k].wait_recv()
            total = total + stat_x[1, k]
        stat_y[0] = total
        for k in range(1, ny):
            got_y[k] = start(
                remote(
                    stat_y.at[0],
                    stat_y.at[k],
                    marks["stat_y"] + k,
                    device(y=(y + k) % ny),
                )
            )
        count = nq + 1
        images = nx * rows
        group[:count] = total[:count] / images
        low_pair[0] = jnp.zeros((8, lanes), F32)
        got_h, got_low = {}, {}

        def half_moments():
            total = stat_y[0]
            for k in range(1, ny):
                got_y[k].wait_recv()
                total = total + stat_y[k]
            stat_h[0] = total
            got_h[0] = start(
                remote(stat_h.at[0], stat_h.at[1], marks["stat_h"], device(h=1 - h))
            )

        def all_moments():
            got_h[0].wait_recv()
            ours, theirs = stat_h[0], stat_h[1]
            total = (ours + theirs) / p.batch
            center = total[:count]
            inverse = lax.rsqrt(total[count:] - center * center + EPS)
            mean[:count] = center
            mean[count:] = inverse
            half_mean = ours[:count] / (images * ny)
            apart = half_mean - theirs[:count] / (images * ny)
            shifts = [stat_y[k][:count] / images - half_mean for k in range(ny)]
            fill = [jnp.zeros((16 - ny - 2, lanes), F32)] if ny < 14 else []
            for q in range(count):
                table = jnp.concatenate(
                    [v[q : q + 1] for v in shifts]
                    + [apart[q : q + 1], inverse[q : q + 1]]
                    + fill,
                    axis=0,
                )
                if q < nq:
                    shift_b[q] = table
                else:
                    column[...] = jnp.transpose(table)

        lane = lax.broadcasted_iota(jnp.int32, (rows, lanes), 1)

        def normal(raw, which):
            v = raw.astype(F32)
            return (v - mean[which : which + 1, :]) * mean[
                count + which : count + which + 1, :
            ]

        def centred(raw, which):
            return raw.astype(F32) - group[which : which + 1, :]

        def center_a():
            for k in range(1, nx):
                into_a[k].wait_recv()
            for i in range(nx):
                low_t[:, i * rows : (i + 1) * rows] = jnp.transpose(
                    centred(raw_a[i], nq)
                ).astype(BF16)

        def normalise(which):
            def low_step(i, _):
                if which < nq:
                    value = normal(raw_b[which, i], which).astype(BF16)
                    low_b[which, i] = value
                else:
                    value = normal(raw_a[i], which).astype(BF16)
                    low_a[i] = value
                low_pair[0, which : which + 1] += jnp.sum(
                    value.astype(F32), axis=0, keepdims=True
                )
                return 0

            lax.fori_loop(0, nx, low_step, 0)

        def low_over_y():
            low_sum[0] = low_pair[0]
            for k in range(1, ny):
                got_low[k] = start(
                    remote(
                        low_sum.at[0],
                        low_sum.at[k],
                        marks["low_y"] + k,
                        device(y=(y + k) % ny),
                    )
                )

        def low_over_h():
            total = low_sum[0]
            for k in range(1, ny):
                got_low[k].wait_recv()
                total = total + low_sum[k]
            half_low[...] = total
            got_low[0] = start(
                remote(half_low, low_pair.at[1], marks["low_h"], device(h=1 - h))
            )

        low_mean = {}

        def low_means():
            got_low[0].wait_recv()
            value = (half_low[...] + low_pair[1]) / p.batch
            low_mean["row"] = value
            low_mean["column"] = jnp.transpose(value)[:, nq : nq + 1]

        passed_z, passed, swaps, pairs = {}, {}, {}, {}
        mid, fin, near_ag, far_ag = {}, {}, {}, {}

        def pass_z(q):
            pass

        def pass_core(q):
            for k in range(1, nx):
                into_b[q, k].wait_recv()
                s = (x + nx - k) % nx
                passed[q, k] = start(
                    remote(
                        raw_b.at[q, s, core_rows],
                        raw_b.at[q, s, core_rows],
                        marks["pass_c"] + q * nx + k,
                        device(core=1 - core),
                    )
                )

        flip = 1 - 2 * (core % 2)

        def along(distance):
            return (y + flip * distance + ny) % ny

        def make_tile(q):
            mine[q].wait()
            for k in range(1, nx):
                passed[q, k].wait_recv()

            def low_b_step(i, _):
                low_b[q, i] = centred(raw_b[q, i], q).astype(BF16)
                return 0

            lax.fori_loop(0, nx, low_b_step, 0)
            product = jnp.dot(
                low_t[...],
                low_b[q].reshape(nx * rows, lanes),
                preferred_element_type=F32,
            )
            tile[q] = product.astype(BF16).reshape(ny, slot, lanes)
            for r, (step, near, goes_on) in enumerate(routes):
                mark = r * nq + q
                if goes_on:
                    t = along(step * (near + 1))
                    mid[r, q] = start(
                        remote(
                            tile.at[q, t],
                            mid_in.at[r, q],
                            marks["mid"] + mark,
                            device(y=along(step)),
                        )
                    )
                else:
                    t = along(step * near)
                    fin[r, q] = start(
                        remote(
                            tile.at[q, t],
                            fin_in.at[r, q],
                            marks["fin"] + mark,
                            device(y=t),
                        )
                    )

        def sum_step(q):
            for r, (step, near, goes_on) in enumerate(routes):
                if goes_on:
                    t = along(step * near)
                    mid[r, q].wait_recv()
                    mid_out[r, q] = (
                        mid_in[r, q].astype(F32) + tile[q, t].astype(F32)
                    ).astype(BF16)
                    fin[r, q] = start(
                        remote(
                            mid_out.at[r, q],
                            fin_in.at[r, q],
                            marks["fin"] + r * nq + q,
                            device(y=t),
                        )
                    )

        own_slot = pl.ds(pl.multiple_of(y * slot, 8), slot)

        def swap_step(q):
            value = tile[q, y].astype(F32)
            for r in range(len(routes)):
                fin[r, q].wait_recv()
                value = value + fin_in[r, q].astype(F32)
            spread = jnp.zeros((slot, lanes), F32)
            for k in range(ny):
                spread += column[own_slot, k : k + 1] * shift_b[q, k : k + 1]
            value = value + images * spread
            owned[q] = value
            swap_out[q] = value.astype(BF16)
            swaps[q] = start(
                remote(
                    swap_out.at[q], swap_in.at[q], marks["swap"] + q, device(h=1 - h)
                )
            )

        def grad_step(q):
            swaps[q].wait_recv()
            spread = column[own_slot, ny : ny + 1] * shift_b[q, ny : ny + 1]
            corr = owned[q] + swap_in[q].astype(F32) + (p.batch / 4) * spread
            scale = column[own_slot, ny + 1 : ny + 2] * shift_b[q, ny + 1 : ny + 2]
            corr = corr * scale / p.batch
            row = y * slot + lax.broadcasted_iota(jnp.int32, (slot, lanes), 0)
            col = lax.broadcasted_iota(jnp.int32, (slot, lanes), 1)
            on = (row == col) & (fs == nq * x + q)
            grad[q, y] = jnp.where(
                on, -2.0 * (1.0 - corr), 2.0 * WEIGHT * corr
            ).astype(BF16)
            for r, (step, near, goes_on) in enumerate(routes):
                near_ag[r, q] = start(
                    remote(
                        grad.at[q, y],
                        grad.at[q, y],
                        marks["near"] + r * nq + q,
                        device(y=along(step * near)),
                    )
                )

        def gather_step(q):
            for r, (step, near, goes_on) in enumerate(routes):
                near_ag[r, q].wait_recv()
                if goes_on:
                    t = along(-step * near)
                    far_ag[r, q] = start(
                        remote(
                            grad.at[q, t],
                            grad.at[q, t],
                            marks["far"] + r * nq + q,
                            device(y=along(step)),
                        )
                    )

        means_a = [jnp.zeros((1, lanes), F32), jnp.zeros((1, lanes), F32)]

        def back_step(q):
            for r, (step, near, goes_on) in enumerate(routes):
                if goes_on:
                    far_ag[r, q].wait_recv()
            row = lax.broadcasted_iota(jnp.int32, (lanes, lanes), 0)
            col = lax.broadcasted_iota(jnp.int32, (lanes, lanes), 1)
            g = grad[q].reshape(lanes, lanes).astype(F32)
            mean_b = low_mean["row"][q : q + 1]
            mean_a = low_mean["column"]
            g = jnp.where((row < block) & (col < block), g, 0.0)
            on = (row == col) & (fs == nq * x + q)
            cross = g * jnp.where(on, 1.0 + 0.5 * g, g / (2.0 * WEIGHT))
            flat_b = jnp.sum(g * mean_a, axis=0, keepdims=True)
            cross_b = jnp.sum(cross, axis=0, keepdims=True)
            low_g = g.astype(BF16)

            def back_b_step(i, _):
                value = jnp.dot(low_a[i], low_g, preferred_element_type=F32)
                value = value - flat_b - normal(raw_b[q, i], q) * cross_b
                blocks[i, q] = (value * mean[count + q : count + q + 1, :]).astype(BF16)
                return 0

            lax.fori_loop(0, nx, back_b_step, 0)
            for m in range(nx // nc):
                pairs[m, q] = start(
                    remote(
                        blocks.at[m * nc + 1 - core, q],
                        pair.at[m, q],
                        marks["pair"] + m * nq + q,
                        device(core=1 - core),
                    )
                )

            means_a[0] += jnp.sum(jnp.transpose(g * mean_b), axis=0, keepdims=True)
            means_a[1] += jnp.sum(jnp.transpose(cross), axis=0, keepdims=True)

            def back_a_step(i, _):
                value = lax.dot_general(
                    low_b[q, i],
                    low_g,
                    (((1,), (1,)), ((), ())),
                    preferred_element_type=F32,
                )
                acc_a[i] = value if q == 0 else acc_a[i] + value
                return 0

            lax.fori_loop(0, nx, back_a_step, 0)

        backs = {}

        def close_a():
            inv_a = mean[count + nq : count + nq + 1, :]

            def close_a_step(i, _):
                value = acc_a[i] - means_a[0] - normal(raw_a[i], nq) * means_a[1]
                value = value * inv_a
                acc_a[i] = value
                send_a[i] = value.astype(BF16)
                return 0

            lax.fori_loop(0, nx, close_a_step, 0)
            for k in range(1, nx):
                t = (x + k) % nx
                backs[k] = start(
                    remote(
                        send_a.at[t], recv_a.at[k], marks["back_a"] + k, device(x=t)
                    )
                )

        mine_f = [nq * x + q for q in range(nq)]

        def scatter_copy(m, q):
            return remote(
                scatter_out.at[m, q],
                line.at[mine_f[q] // nc],
                marks["scatter"] + q * pairs_x + m,
                device(x=m * nc + core, core=mine_f[q] % nc),
                marks["scatter"] + q * nx + x,
            )

        def stays(m, q):
            return (m * nc + core == x) & (mine_f[q] % nc == core)

        def scatter_step(q):
            for m in range(pairs_x):
                pairs[m, q].wait_recv()
                value = blocks[m * nc + core, q].astype(F32) + pair[m, q].astype(F32)
                value = value.astype(BF16).reshape(SUB, part, lanes)

                @pl.when(stays(m, q))
                def _():
                    line[mine_f[q] // nc] = value

                @pl.when(jnp.logical_not(stays(m, q)))
                def _():
                    scatter_out[m, q] = value
                    scatter_copy(m, q).start()

        middle = nz // 2
        low_half = zl < middle

        def chain_copy(kind, d, s, there):
            return remote(
                chain_out.at[d, s],
                chain_in.at[kind, d, s],
                marks["chain"] + d * SUB + s,
                device(zl=there),
                marks["chain"] + (kind * nz + d) * SUB + s,
            )

        def chain_place(d):
            same = low_half if d < middle else jnp.logical_not(low_half)
            first, end = (0, middle - 1) if d < middle else (middle, nz - 1)
            up = zl < d
            kind = jnp.where(same, jnp.where(up, 0, 1), 2)
            edge = jnp.where(low_half, middle - 1, middle)
            beside = jnp.where(up, zl + 1, zl - 1)
            there = jnp.where(jnp.logical_not(same) & (zl == edge), d, beside)
            level = jnp.where(
                same,
                jnp.where(up, zl - first, end - zl),
                jnp.where(low_half, zl, nz - 1 - zl),
            )
            return kind, there, level

        def chain_step(q, s_x, at_level):
            f = nq * s_x + q
            d = f // nc
            kind, there, level = chain_place(d)

            if at_level == 0:

                @pl.when(
                    (core == f % nc)
                    & jnp.logical_not((x == s_x) & (core == x % nc))
                )
                def _():
                    remote(
                        scatter_out.at[0, q],
                        line.at[d],
                        marks["scatter"],
                        device(core=1 - core),
                        marks["scatter"] + q * nx + s_x,
                    ).wait_recv()

            @pl.when((core == f % nc) & (zl != d) & (level == at_level))
            def _():
                for s in range(SUB):
                    if at_level == 0:
                        chain_out[d, s] = line[d, s]
                    else:
                        chain_copy(kind, d, s, there).wait_recv()
                        chain_out[d, s] = (
                            line[d, s].astype(F32) + chain_in[kind, d, s].astype(F32)
                        ).astype(BF16)
                    chain_copy(kind, d, s, there).start()

        tasks = []

        def at(time, what, *which):
            tasks.append((time, len(tasks), what, which))

        at(7.5, center_a)
        at(12.6, half_moments)
        at(23.0, all_moments)
        at(24.2, normalise, nq)
        at(28.2, low_over_y)
        at(34.0, low_over_h)
        at(41.3, low_means)
        for q in range(nq):
            at(11.0 + 2.3 * q, pass_z, q)
            at(12.0 + 3.7 * q, pass_core, q)
            at(13.5 + 3.7 * q, make_tile, q)
            at((24.4, 24.6, 28.0)[q] if nq == 3 else 28.0, normalise, q)
            now = 18.5 + 3.7 * q
            at(now, sum_step, q)
            at(now + 5.5, swap_step, q)
            at(now + 13.5, grad_step, q)
            at(now + 19.0, gather_step, q)
            now += 23.0
            at(now, back_step, q)
            now += 2.0
            at(now, scatter_step, q)
            if q == nq - 1:
                at(now, close_a)
            for level in range(middle):
                for s_x in range(nx):
                    at(now + 5.0 + 2.5 * level, chain_step, q, s_x, level)
        for _, _, what, which in sorted(tasks, key=lambda task: task[:2]):
            what(*which)

        total_a = acc_a[x]
        for k in range(1, nx):
            backs[k].wait_recv()
            total_a = total_a + recv_a[k].astype(F32)
        out[0] = total_a.astype(BF16)

        here = jnp.where(low_half, zl, zl - middle)
        beside_me = (zl + 1) % nz
        for s in range(SUB):
            owned_b[...] = line[zl, s].astype(F32)
            chain_copy(2, zl, s, beside_me).wait_recv()
            owned_b[...] += chain_in[2, zl, s].astype(F32)

            @pl.when(here > 0)
            def _():
                chain_copy(0, zl, s, beside_me).wait_recv()
                owned_b[...] += chain_in[0, zl, s].astype(F32)

            @pl.when(here < middle - 1)
            def _():
                chain_copy(1, zl, s, beside_me).wait_recv()
                owned_b[...] += chain_in[1, zl, s].astype(F32)

            out[1, s * part : (s + 1) * part] = owned_b[...].astype(BF16)

        for q in range(nq):
            for m in range(pairs_x):

                @pl.when(jnp.logical_not(stays(m, q)))
                def _():
                    scatter_copy(m, q).wait_send()

        for d in range(nz):

            @pl.when(zl != d)
            def _():
                kind, there, _ = chain_place(d)
                for s in range(SUB):
                    chain_copy(kind, d, s, there).wait_send()

        for copy in waiting:
            copy.wait_send()

    vmem = pltpu.VMEM
    count = nq + 1
    shapes = [
        vmem((nx, rows, lanes), BF16),
        vmem((nq, nx, rows, lanes), BF16),
        vmem((nx, nq, rows, lanes), BF16),
        vmem((nx, rows, lanes), BF16),
        vmem((nq, nx, rows, lanes), BF16),
        vmem((lanes, nx * rows), BF16),
        vmem((2, nx, 2 * count, lanes), F32),
        vmem((ny, 2 * count, lanes), F32),
        vmem((2, 2 * count, lanes), F32),
        vmem((ny, 8, lanes), F32),
        vmem((2, 8, lanes), F32),
        vmem((8, lanes), F32),
        vmem((8, lanes), F32),
        vmem((2 * count, lanes), F32),
        vmem((nq, 16, lanes), F32),
        vmem((lanes, 16), F32),
        vmem((nq, ny, slot, lanes), BF16),
        vmem((len(routes), nq, slot, lanes), BF16),
        vmem((len(routes), nq, slot, lanes), BF16),
        vmem((len(routes), nq, slot, lanes), BF16),
        vmem((nq, slot, lanes), F32),
        vmem((nq, slot, lanes), BF16),
        vmem((nq, slot, lanes), BF16),
        vmem((nq, ny, slot, lanes), BF16),
        vmem((nx, rows, lanes), F32),
        vmem((nx, rows, lanes), BF16),
        vmem((nx, rows, lanes), BF16),
        vmem((nx, nq, rows, lanes), BF16),
        vmem((nx // nc, nq, rows, lanes), BF16),
        vmem((pairs_x, nq, SUB, part, lanes), BF16),
        vmem((nz, SUB, part, lanes), BF16),
        vmem((3, nz, SUB, part, lanes), BF16),
        vmem((nz, SUB, part, lanes), BF16),
        vmem((part, lanes), F32),
        pltpu.SemaphoreType.DMA((copies.count,)),
        pltpu.SemaphoreType.DMA((copies.count,)),
        pltpu.SemaphoreType.DMA((nq,)),
    ]
    result = jax.ShapeDtypeStruct((2, rows, lanes), BF16)
    return pl.pallas_call(
        kernel,
        out_shape=result,
        in_specs=[pl.BlockSpec(memory_space=vmem)] * 2,
        out_specs=pl.BlockSpec(memory_space=vmem),
        scratch_shapes=shapes,
        compiler_params=pltpu.CompilerParams(
            collective_id=0, has_side_effects=True, vmem_limit_bytes=56 << 20
        ),
    )


def solution(mesh):
    def local(z_a, z_b):
        grads = build(Plan(mesh, *z_a.shape))(z_a, z_b)
        block = z_a.shape[1]
        return grads[0, :, :block], grads[1, :, :block]

    return jax.shard_map(
        local,
        mesh=mesh,
        in_specs=(P("dp", "fsdp"), P("dp", None)),
        out_specs=(P("dp", "fsdp"), P("dp", "fsdp")),
        check_vma=False,
    )
```

```python
import jax
import jax.numpy as jnp
from jax import lax
from jax.experimental import pallas as pl
from jax.experimental.pallas import tpu as pltpu
from jax.sharding import PartitionSpec as P

EPS = 1e-05
WEIGHT = 0.0051
LANES = 128
CORES = 2
Z_HI = 2
X_CHIPS = 4
SUB = 4
MESH = pl.DeviceIdType.MESH
F32 = jnp.float32
BF16 = jnp.bfloat16


class Plan:
    def __init__(self, mesh, rows, block):
        fsdp, dp = mesh.shape["fsdp"], mesh.shape["dp"]
        self.nx, self.nh, self.nc = X_CHIPS, Z_HI, CORES
        self.ny = dp // (self.nx * self.nh)
        self.nz = fsdp // self.nc
        self.nf = fsdp
        self.nq = self.nf // self.nx
        self.rows, self.block = rows, block
        self.lanes = -(-(block + 1) // LANES) * LANES
        self.slot = self.lanes // self.ny
        self.batch = rows * dp
        right = self.ny // 2
        self.routes = []
        for step, reach in ((1, right), (-1, self.ny - 1 - right)):
            for near in range(1, reach + 1, 2):
                self.routes.append((step, near, near < reach))
        self.routes.sort(key=lambda route: -route[1])


class Copies:
    def __init__(self):
        self.count = 0

    def take(self, n=1):
        first = self.count
        self.count += n
        return first


def build(p):
    copies = Copies()
    nx, ny, nh, nz, nc, nq = p.nx, p.ny, p.nh, p.nz, p.nc, p.nq
    rows, lanes, slot, block = p.rows, p.lanes, p.slot, p.block
    half = rows // nc
    quarter = half // 2
    part = rows // SUB
    routes = p.routes
    pairs_x = nx // nc
    marks = dict(
        a=copies.take(nx),
        b=copies.take(nx * nq),
        pass_z=copies.take(nx * nq),
        pass_c=copies.take(nx * nq),
        stat_x=copies.take(nx),
        stat_y=copies.take(ny),
        stat_h=copies.take(1),
        low_y=copies.take(ny),
        low_h=copies.take(1),
        mid=copies.take(len(routes) * nq),
        fin=copies.take(len(routes) * nq),
        swap=copies.take(nq),
        near=copies.take(len(routes) * nq),
        far=copies.take(len(routes) * nq),
        pair=copies.take(pairs_x * nq),
        back_a=copies.take(nx),
        scatter=copies.take(max(pairs_x, nx) * nq),
        chain=copies.take(3 * nz * SUB),
    )

    def kernel(
        za,
        zb,
        out,
        raw_a,
        raw_b,
        pack,
        low_a,
        low_b,
        low_t,
        stat_x,
        stat_y,
        stat_h,
        low_sum,
        low_pair,
        half_low,
        group,
        mean,
        shift_b,
        column,
        tile,
        mid_in,
        mid_out,
        fin_in,
        owned,
        swap_out,
        swap_in,
        grad,
        acc_a,
        send_a,
        recv_a,
        blocks,
        pair,
        scatter_out,
        line,
        chain_in,
        chain_out,
        owned_b,
        send_sem,
        recv_sem,
        own_sem,
    ):
        dp = lax.axis_index("dp")
        fs = lax.axis_index("fsdp")
        x = dp % nx
        h = (dp // nx) % nh
        y = dp // (nx * nh)
        core = fs % nc
        zl = fs // nc

        def device(x=x, y=y, h=h, zl=zl, core=core):
            return {"dp": (y * nh + h) * nx + x, "fsdp": zl * nc + core}

        def remote(src, dst, mark, there, recv_mark=None):
            arrived = mark if recv_mark is None else recv_mark
            return pltpu.make_async_remote_copy(
                src_ref=src,
                dst_ref=dst,
                send_sem=send_sem.at[mark],
                recv_sem=recv_sem.at[arrived],
                device_id=there,
                device_id_type=MESH,
            )

        barrier = pltpu.get_barrier_semaphore()

        def greet(there):
            pl.semaphore_signal(barrier, inc=1, device_id=there, device_id_type=MESH)

        greet(device(core=1 - core))
        for k in range(1, nx):
            greet(device(x=(x + k) % nx))
            greet(device(x=(x + k) % nx, core=1 - core))
        for k in range(1, ny):
            greet(device(y=(y + k) % ny))
        greet(device(h=1 - h))
        for k in range(1, nz):
            greet(device(zl=(zl + k) % nz))

        waiting = []

        zero = jnp.zeros((rows, lanes - block), BF16)
        raw_a[x] = jnp.concatenate([za[...], zero], axis=1)
        for f in range(p.nf):
            piece = zb[:, f * block : (f + 1) * block]
            pack[f // nq, f % nq] = jnp.concatenate([piece, zero], axis=1)

        def sums(value):
            v = value.astype(F32)
            return (
                jnp.sum(v, axis=0, keepdims=True),
                jnp.sum(v * v, axis=0, keepdims=True),
            )

        first = [sums(pack[f // nq, f % nq]) for f in range(p.nf)]
        first_a = sums(raw_a[x])
        for t in range(nx):
            both = first[t * nq : (t + 1) * nq] + [first_a]
            stat_x[0, t] = jnp.concatenate(
                [s for s, _ in both] + [s for _, s in both], axis=0
            )

        pl.semaphore_wait(barrier, 2 * (nx - 1) + ny - 1 + nz - 1 + 2)

        def start(copy):
            copy.start()
            waiting.append(copy)
            return copy

        got_x, got_y = {}, {}
        for k in range(1, nx):
            t = (x + k) % nx
            got_x[k] = start(
                remote(
                    stat_x.at[0, t],
                    stat_x.at[1, k],
                    marks["stat_x"] + k,
                    device(x=t),
                )
            )
        into_a = {}
        for k in range(1, nx):
            into_a[k] = start(
                remote(
                    raw_a.at[x], raw_a.at[x], marks["a"] + k, device(x=(x + k) % nx)
                )
            )
        own_rows = pl.ds(core * half, half)
        core_rows = pl.ds(core * half, half)
        z_pair = device(zl=zl + 1 - 2 * (zl % 2))
        into_b = {}
        for q in range(nq):
            for k in range(1, nx):
                t = (x + k) % nx
                into_b[q, k] = start(
                    remote(
                        pack.at[t, q, own_rows],
                        raw_b.at[q, x, own_rows],
                        marks["b"] + q * nx + k,
                        device(x=t),
                    )
                )
        mine = []
        for q in range(nq):
            copy = pltpu.make_async_copy(pack.at[x, q], raw_b.at[q, x], own_sem.at[q])
            copy.start()
            mine.append(copy)

        total = stat_x[0, x]
        for k in range(1, nx):
            got_x[k].wait_recv()
            total = total + stat_x[1, k]
        stat_y[0] = total
        for k in range(1, ny):
            got_y[k] = start(
                remote(
                    stat_y.at[0],
                    stat_y.at[k],
                    marks["stat_y"] + k,
                    device(y=(y + k) % ny),
                )
            )
        count = nq + 1
        images = nx * rows
        group[:count] = total[:count] / images
        low_pair[0] = jnp.zeros((8, lanes), F32)
        got_h, got_low = {}, {}

        def half_moments():
            total = stat_y[0]
            for k in range(1, ny):
                got_y[k].wait_recv()
                total = total + stat_y[k]
            stat_h[0] = total
            got_h[0] = start(
                remote(stat_h.at[0], stat_h.at[1], marks["stat_h"], device(h=1 - h))
            )

        def all_moments():
            got_h[0].wait_recv()
            ours, theirs = stat_h[0], stat_h[1]
            total = (ours + theirs) / p.batch
            center = total[:count]
            inverse = lax.rsqrt(total[count:] - center * center + EPS)
            mean[:count] = center
            mean[count:] = inverse
            half_mean = ours[:count] / (images * ny)
            apart = half_mean - theirs[:count] / (images * ny)
            shifts = [stat_y[k][:count] / images - half_mean for k in range(ny)]
            fill = [jnp.zeros((16 - ny - 2, lanes), F32)] if ny < 14 else []
            for q in range(count):
                table = jnp.concatenate(
                    [v[q : q + 1] for v in shifts]
                    + [apart[q : q + 1], inverse[q : q + 1]]
                    + fill,
                    axis=0,
                )
                if q < nq:
                    shift_b[q] = table
                else:
                    column[...] = jnp.transpose(table)

        lane = lax.broadcasted_iota(jnp.int32, (rows, lanes), 1)

        def normal(raw, which):
            v = raw.astype(F32)
            return (v - mean[which : which + 1, :]) * mean[
                count + which : count + which + 1, :
            ]

        def centred(raw, which):
            return raw.astype(F32) - group[which : which + 1, :]

        def center_a():
            for k in range(1, nx):
                into_a[k].wait_recv()
            for i in range(nx):
                low_t[:, i * rows : (i + 1) * rows] = jnp.transpose(
                    centred(raw_a[i], nq)
                ).astype(BF16)

        def normalise(which):
            def low_step(i, _):
                if which < nq:
                    value = normal(raw_b[which, i], which).astype(BF16)
                    low_b[which, i] = value
                else:
                    value = normal(raw_a[i], which).astype(BF16)
                    low_a[i] = value
                low_pair[0, which : which + 1] += jnp.sum(
                    value.astype(F32), axis=0, keepdims=True
                )
                return 0

            lax.fori_loop(0, nx, low_step, 0)

        def low_over_y():
            low_sum[0] = low_pair[0]
            for k in range(1, ny):
                got_low[k] = start(
                    remote(
                        low_sum.at[0],
                        low_sum.at[k],
                        marks["low_y"] + k,
                        device(y=(y + k) % ny),
                    )
                )

        def low_over_h():
            total = low_sum[0]
            for k in range(1, ny):
                got_low[k].wait_recv()
                total = total + low_sum[k]
            half_low[...] = total
            got_low[0] = start(
                remote(half_low, low_pair.at[1], marks["low_h"], device(h=1 - h))
            )

        low_mean = {}

        def low_means():
            got_low[0].wait_recv()
            value = (half_low[...] + low_pair[1]) / p.batch
            low_mean["row"] = value
            low_mean["column"] = jnp.transpose(value)[:, nq : nq + 1]

        passed_z, passed, swaps, pairs = {}, {}, {}, {}
        mid, fin, near_ag, far_ag = {}, {}, {}, {}

        def pass_z(q):
            pass

        def pass_core(q):
            for k in range(1, nx):
                into_b[q, k].wait_recv()
                s = (x + nx - k) % nx
                passed[q, k] = start(
                    remote(
                        raw_b.at[q, s, core_rows],
                        raw_b.at[q, s, core_rows],
                        marks["pass_c"] + q * nx + k,
                        device(core=1 - core),
                    )
                )

        flip = 1 - 2 * (core % 2)

        def along(distance):
            return (y + flip * distance + ny) % ny

        def make_tile(q):
            mine[q].wait()
            for k in range(1, nx):
                passed[q, k].wait_recv()

            def low_b_step(i, _):
                low_b[q, i] = centred(raw_b[q, i], q).astype(BF16)
                return 0

            lax.fori_loop(0, nx, low_b_step, 0)
            product = jnp.dot(
                low_t[...],
                low_b[q].reshape(nx * rows, lanes),
                preferred_element_type=F32,
            )
            tile[q] = product.astype(BF16).reshape(ny, slot, lanes)
            for r, (step, near, goes_on) in enumerate(routes):
                mark = r * nq + q
                if goes_on:
                    t = along(step * (near + 1))
                    mid[r, q] = start(
                        remote(
                            tile.at[q, t],
                            mid_in.at[r, q],
                            marks["mid"] + mark,
                            device(y=along(step)),
                        )
                    )
                else:
                    t = along(step * near)
                    fin[r, q] = start(
                        remote(
                            tile.at[q, t],
                            fin_in.at[r, q],
                            marks["fin"] + mark,
                            device(y=t),
                        )
                    )

        def sum_step(q):
            for r, (step, near, goes_on) in enumerate(routes):
                if goes_on:
                    t = along(step * near)
                    mid[r, q].wait_recv()
                    mid_out[r, q] = (
                        mid_in[r, q].astype(F32) + tile[q, t].astype(F32)
                    ).astype(BF16)
                    fin[r, q] = start(
                        remote(
                            mid_out.at[r, q],
                            fin_in.at[r, q],
                            marks["fin"] + r * nq + q,
                            device(y=t),
                        )
                    )

        own_slot = pl.ds(pl.multiple_of(y * slot, 8), slot)

        def swap_step(q):
            value = tile[q, y].astype(F32)
            for r in range(len(routes)):
                fin[r, q].wait_recv()
                value = value + fin_in[r, q].astype(F32)
            spread = jnp.zeros((slot, lanes), F32)
            for k in range(ny):
                spread += column[own_slot, k : k + 1] * shift_b[q, k : k + 1]
            value = value + images * spread
            owned[q] = value
            swap_out[q] = value.astype(BF16)
            swaps[q] = start(
                remote(
                    swap_out.at[q], swap_in.at[q], marks["swap"] + q, device(h=1 - h)
                )
            )

        def grad_step(q):
            swaps[q].wait_recv()
            spread = column[own_slot, ny : ny + 1] * shift_b[q, ny : ny + 1]
            corr = owned[q] + swap_in[q].astype(F32) + (p.batch / 4) * spread
            scale = column[own_slot, ny + 1 : ny + 2] * shift_b[q, ny + 1 : ny + 2]
            corr = corr * scale / p.batch
            row = y * slot + lax.broadcasted_iota(jnp.int32, (slot, lanes), 0)
            col = lax.broadcasted_iota(jnp.int32, (slot, lanes), 1)
            on = (row == col) & (fs == nq * x + q)
            grad[q, y] = jnp.where(
                on, -2.0 * (1.0 - corr), 2.0 * WEIGHT * corr
            ).astype(BF16)
            for r, (step, near, goes_on) in enumerate(routes):
                near_ag[r, q] = start(
                    remote(
                        grad.at[q, y],
                        grad.at[q, y],
                        marks["near"] + r * nq + q,
                        device(y=along(step * near)),
                    )
                )

        def gather_step(q):
            for r, (step, near, goes_on) in reversed(list(enumerate(routes))):
                near_ag[r, q].wait_recv()
                if goes_on:
                    t = along(-step * near)
                    far_ag[r, q] = start(
                        remote(
                            grad.at[q, t],
                            grad.at[q, t],
                            marks["far"] + r * nq + q,
                            device(y=along(step)),
                        )
                    )

        means_a = [jnp.zeros((1, lanes), F32), jnp.zeros((1, lanes), F32)]

        def back_step(q):
            for r, (step, near, goes_on) in enumerate(routes):
                if goes_on:
                    far_ag[r, q].wait_recv()
            row = lax.broadcasted_iota(jnp.int32, (lanes, lanes), 0)
            col = lax.broadcasted_iota(jnp.int32, (lanes, lanes), 1)
            g = grad[q].reshape(lanes, lanes).astype(F32)
            mean_b = low_mean["row"][q : q + 1]
            mean_a = low_mean["column"]
            g = jnp.where((row < block) & (col < block), g, 0.0)
            on = (row == col) & (fs == nq * x + q)
            cross = g * jnp.where(on, 1.0 + 0.5 * g, g / (2.0 * WEIGHT))
            flat_b = jnp.sum(g * mean_a, axis=0, keepdims=True)
            cross_b = jnp.sum(cross, axis=0, keepdims=True)
            low_g = g.astype(BF16)

            def back_b_step(i, _):
                value = jnp.dot(low_a[i], low_g, preferred_element_type=F32)
                value = value - flat_b - normal(raw_b[q, i], q) * cross_b
                blocks[i, q] = (value * mean[count + q : count + q + 1, :]).astype(BF16)
                return 0

            lax.fori_loop(0, nx, back_b_step, 0)
            for m in range(nx // nc):
                pairs[m, q] = start(
                    remote(
                        blocks.at[m * nc + 1 - core, q],
                        pair.at[m, q],
                        marks["pair"] + m * nq + q,
                        device(core=1 - core),
                    )
                )

            means_a[0] += jnp.sum(jnp.transpose(g * mean_b), axis=0, keepdims=True)
            means_a[1] += jnp.sum(jnp.transpose(cross), axis=0, keepdims=True)

            def back_a_step(i, _):
                value = lax.dot_general(
                    low_b[q, i],
                    low_g,
                    (((1,), (1,)), ((), ())),
                    preferred_element_type=F32,
                )
                acc_a[i] = value if q == 0 else acc_a[i] + value
                return 0

            lax.fori_loop(0, nx, back_a_step, 0)

        backs = {}

        def close_a():
            inv_a = mean[count + nq : count + nq + 1, :]

            def close_a_step(i, _):
                value = acc_a[i] - means_a[0] - normal(raw_a[i], nq) * means_a[1]
                value = value * inv_a
                acc_a[i] = value
                send_a[i] = value.astype(BF16)
                return 0

            lax.fori_loop(0, nx, close_a_step, 0)
            for k in range(1, nx):
                t = (x + k) % nx
                backs[k] = start(
                    remote(
                        send_a.at[t], recv_a.at[k], marks["back_a"] + k, device(x=t)
                    )
                )

        mine_f = [nq * x + q for q in range(nq)]

        def scatter_copy(m, q):
            return remote(
                scatter_out.at[m, q],
                line.at[mine_f[q] // nc],
                marks["scatter"] + q * pairs_x + m,
                device(x=m * nc + core, core=mine_f[q] % nc),
                marks["scatter"] + q * nx + x,
            )

        def stays(m, q):
            return (m * nc + core == x) & (mine_f[q] % nc == core)

        def scatter_step(q):
            for m in range(pairs_x):
                pairs[m, q].wait_recv()
                value = blocks[m * nc + core, q].astype(F32) + pair[m, q].astype(F32)
                value = value.astype(BF16).reshape(SUB, part, lanes)

                @pl.when(stays(m, q))
                def _():
                    line[mine_f[q] // nc] = value

                @pl.when(jnp.logical_not(stays(m, q)))
                def _():
                    scatter_out[m, q] = value
                    scatter_copy(m, q).start()

        middle = nz // 2
        low_half = zl < middle

        def chain_copy(kind, d, s, there):
            return remote(
                chain_out.at[d, s],
                chain_in.at[kind, d, s],
                marks["chain"] + d * SUB + s,
                device(zl=there),
                marks["chain"] + (kind * nz + d) * SUB + s,
            )

        def chain_place(d):
            same = low_half if d < middle else jnp.logical_not(low_half)
            first, end = (0, middle - 1) if d < middle else (middle, nz - 1)
            up = zl < d
            kind = jnp.where(same, jnp.where(up, 0, 1), 2)
            edge = jnp.where(low_half, middle - 1, middle)
            beside = jnp.where(up, zl + 1, zl - 1)
            there = jnp.where(jnp.logical_not(same) & (zl == edge), d, beside)
            level = jnp.where(
                same,
                jnp.where(up, zl - first, end - zl),
                jnp.where(low_half, zl, nz - 1 - zl),
            )
            return kind, there, level

        def chain_step(q, s_x, at_level):
            f = nq * s_x + q
            d = f // nc
            kind, there, level = chain_place(d)

            if at_level == 0:

                @pl.when(
                    (core == f % nc)
                    & jnp.logical_not((x == s_x) & (core == x % nc))
                )
                def _():
                    remote(
                        scatter_out.at[0, q],
                        line.at[d],
                        marks["scatter"],
                        device(core=1 - core),
                        marks["scatter"] + q * nx + s_x,
                    ).wait_recv()

            @pl.when((core == f % nc) & (zl != d) & (level == at_level))
            def _():
                for s in range(SUB):
                    if at_level == 0:
                        chain_out[d, s] = line[d, s]
                    else:
                        chain_copy(kind, d, s, there).wait_recv()
                        chain_out[d, s] = (
                            line[d, s].astype(F32) + chain_in[kind, d, s].astype(F32)
                        ).astype(BF16)
                    chain_copy(kind, d, s, there).start()

        tasks = []

        def at(time, what, *which):
            tasks.append((time, len(tasks), what, which))

        at(7.5, center_a)
        at(12.6, half_moments)
        at(23.0, all_moments)
        at(24.2, normalise, nq)
        at(28.2, low_over_y)
        at(34.0, low_over_h)
        at(41.3, low_means)
        for q in range(nq):
            at(11.0 + 2.3 * q, pass_z, q)
            at(12.0 + 3.7 * q, pass_core, q)
            at(13.5 + 3.7 * q, make_tile, q)
            at((24.4, 24.6, 28.0)[q] if nq == 3 else 28.0, normalise, q)
            now = 18.5 + 3.7 * q
            at(now, sum_step, q)
            at(now + 5.5, swap_step, q)
            at(now + 13.5, grad_step, q)
            at(now + 19.0, gather_step, q)
            now += 23.0
            at(now, back_step, q)
            now += 2.0
            at(now, scatter_step, q)
            if q == nq - 1:
                at(now, close_a)
            for level in range(middle):
                for s_x in range(nx):
                    at(now + 5.0 + 2.5 * level, chain_step, q, s_x, level)
        for _, _, what, which in sorted(tasks, key=lambda task: task[:2]):
            what(*which)

        total_a = acc_a[x]
        for k in range(1, nx):
            backs[k].wait_recv()
            total_a = total_a + recv_a[k].astype(F32)
        out[0] = total_a.astype(BF16)

        here = jnp.where(low_half, zl, zl - middle)
        beside_me = (zl + 1) % nz
        for s in range(SUB):
            owned_b[...] = line[zl, s].astype(F32)
            chain_copy(2, zl, s, beside_me).wait_recv()
            owned_b[...] += chain_in[2, zl, s].astype(F32)

            @pl.when(here > 0)
            def _():
                chain_copy(0, zl, s, beside_me).wait_recv()
                owned_b[...] += chain_in[0, zl, s].astype(F32)

            @pl.when(here < middle - 1)
            def _():
                chain_copy(1, zl, s, beside_me).wait_recv()
                owned_b[...] += chain_in[1, zl, s].astype(F32)

            out[1, s * part : (s + 1) * part] = owned_b[...].astype(BF16)

        for q in range(nq):
            for m in range(pairs_x):

                @pl.when(jnp.logical_not(stays(m, q)))
                def _():
                    scatter_copy(m, q).wait_send()

        for d in range(nz):

            @pl.when(zl != d)
            def _():
                kind, there, _ = chain_place(d)
                for s in range(SUB):
                    chain_copy(kind, d, s, there).wait_send()

        for copy in waiting:
            copy.wait_send()

    vmem = pltpu.VMEM
    count = nq + 1
    shapes = [
        vmem((nx, rows, lanes), BF16),
        vmem((nq, nx, rows, lanes), BF16),
        vmem((nx, nq, rows, lanes), BF16),
        vmem((nx, rows, lanes), BF16),
        vmem((nq, nx, rows, lanes), BF16),
        vmem((lanes, nx * rows), BF16),
        vmem((2, nx, 2 * count, lanes), F32),
        vmem((ny, 2 * count, lanes), F32),
        vmem((2, 2 * count, lanes), F32),
        vmem((ny, 8, lanes), F32),
        vmem((2, 8, lanes), F32),
        vmem((8, lanes), F32),
        vmem((8, lanes), F32),
        vmem((2 * count, lanes), F32),
        vmem((nq, 16, lanes), F32),
        vmem((lanes, 16), F32),
        vmem((nq, ny, slot, lanes), BF16),
        vmem((len(routes), nq, slot, lanes), BF16),
        vmem((len(routes), nq, slot, lanes), BF16),
        vmem((len(routes), nq, slot, lanes), BF16),
        vmem((nq, slot, lanes), F32),
        vmem((nq, slot, lanes), BF16),
        vmem((nq, slot, lanes), BF16),
        vmem((nq, ny, slot, lanes), BF16),
        vmem((nx, rows, lanes), F32),
        vmem((nx, rows, lanes), BF16),
        vmem((nx, rows, lanes), BF16),
        vmem((nx, nq, rows, lanes), BF16),
        vmem((nx // nc, nq, rows, lanes), BF16),
        vmem((pairs_x, nq, SUB, part, lanes), BF16),
        vmem((nz, SUB, part, lanes), BF16),
        vmem((3, nz, SUB, part, lanes), BF16),
        vmem((nz, SUB, part, lanes), BF16),
        vmem((part, lanes), F32),
        pltpu.SemaphoreType.DMA((copies.count,)),
        pltpu.SemaphoreType.DMA((copies.count,)),
        pltpu.SemaphoreType.DMA((nq,)),
    ]
    result = jax.ShapeDtypeStruct((2, rows, lanes), BF16)
    return pl.pallas_call(
        kernel,
        out_shape=result,
        in_specs=[pl.BlockSpec(memory_space=vmem)] * 2,
        out_specs=pl.BlockSpec(memory_space=vmem),
        scratch_shapes=shapes,
        compiler_params=pltpu.CompilerParams(
            collective_id=0, has_side_effects=True, vmem_limit_bytes=56 << 20
        ),
    )


def solution(mesh):
    def local(z_a, z_b):
        grads = build(Plan(mesh, *z_a.shape))(z_a, z_b)
        block = z_a.shape[1]
        return grads[0, :, :block], grads[1, :, :block]

    return jax.shard_map(
        local,
        mesh=mesh,
        in_specs=(P("dp", "fsdp"), P("dp", None)),
        out_specs=(P("dp", "fsdp"), P("dp", "fsdp")),
        check_vma=False,
    )
```
